256 devices in a mesh: grp: 16 (over x, z_hi, core), tw: 16 (over y, z_lo).
Axes of the slice: x: 4, y: 4, z: 8 (z_hi: 2, z_lo: 4; z = z_hi * 4 + z_lo), core: 2. Of those that a mesh axis runs over, the one named last changes fastest.
Arguments:
- orbitals: bfloat16 [128, 2048, 256], P('tw', 'grp'), may hold values from -1.5 to 1.5
- slab_points: int32 [256], replicated, may hold values from 0 to 2047, as said below
- kernel: bfloat16 [128, 256, 2048], P(None, 'tw', 'grp'), may hold values from -6 to 6
- twist_map: int32 [128, 128], replicated, may hold values from 0 to 127, as said below
Outputs:
- projector: bfloat16 [128, 256, 256], P('tw', 'grp')
The draws below stay inside these ranges and needn't reach their ends.
Inputs may be any that keep to these rules, and one draw needn't show every extreme that they name: `slab_points`: distinct point indices; point 0 and point 2048 - 1 are always among them. The twists are the points of a 4 x 4 x 8 grid in some order; twist_map[k, q] is the twist at the grid difference of k and q, wrapping around each grid dimension.
All inputs are finite; a program needn't handle non-finite values.
Results may differ from the reference program's by a relative error of at most 0.0057.
Values may be sent and summed in bfloat16 or wider, within the bound.
No kernel may reach another device: no remote copies, remote signals or barrier semaphores. Data moves between devices by JAX's collectives and lax.ppermute only.
A program may use at most 64 MiB of HBM per device.

```python
import jax
import jax.numpy as jnp
from jax import lax

NPTS = 2048
NB = 256
SLAB = 256
TWISTS = 128


def draw_slab_points(key, part):
    inner = jax.random.permutation(jax.random.fold_in(key, 11), NPTS - 2).astype(jnp.int32) + 1
    ends = jnp.array([0, NPTS - 1], dtype=jnp.int32)
    chosen = jnp.concatenate([ends, inner[:SLAB - 2]])
    order = jax.random.permutation(jax.random.fold_in(key, 13), SLAB)
    return chosen[order].astype(jnp.int32)


def draw_twist_map(key, part):
    labels = jax.random.permutation(jax.random.fold_in(key, 23), TWISTS).astype(jnp.int32)
    third = TWISTS // 16
    where = jnp.zeros((TWISTS,), jnp.int32).at[labels].set(jnp.arange(TWISTS, dtype=jnp.int32))
    first_c = where // (4 * third)
    second_c = where // third % 4
    third_c = where % third
    diff_a = (first_c[:, None] - first_c[None, :]) % 4
    diff_b = (second_c[:, None] - second_c[None, :]) % 4
    diff_c = (third_c[:, None] - third_c[None, :]) % third
    position = diff_a * (4 * third) + diff_b * third + diff_c
    return labels[position].astype(jnp.int32)


def steps_of(key, extent, shards, smallest, high):
    gain, own = 1.0, jax.random.fold_in(key, 6)
    for dim, blocks in shards:
        draws = jnp.exp(jax.random.uniform(jax.random.fold_in(own, dim), (blocks,), jnp.float32, smallest / len(shards), high / len(shards)))
        gain = gain * jnp.repeat(draws, extent[dim] // blocks).reshape([-1 if axis == dim else 1 for axis in range(len(extent))])
    return gain


def bell_draw(key, dims, width, limit, cuts=(), kind=jnp.bfloat16):
    values = jax.random.normal(key, dims, jnp.float32) * width
    if len(cuts) > 0:
        values = steps_of(key, dims, cuts, -0.22, 0.18) * values
    return jnp.clip(values, min=-limit, max=limit).astype(kind)


def setup_inputs(seed: int = 0) -> dict:
    keys = jax.random.split(jax.random.key(seed), 5)
    return {
        "orbitals": bell_draw(keys[0], (TWISTS, NPTS, NB), 0.25, 1.5, ((0, 16), (1, 16))),
        "slab_points": draw_slab_points(jax.random.fold_in(keys[4], 71), 0),
        "kernel": bell_draw(keys[2], (TWISTS, SLAB, NPTS), 1.0, 6.0, ((1, 16), (2, 16))),
        "twist_map": draw_twist_map(jax.random.fold_in(keys[4], 71), 0),
    }


def reference(orbitals, slab_points, kernel, twist_map):
    picked = jnp.take(orbitals, slab_points.astype(jnp.int32), axis=1)
    pairs = jnp.einsum("ksb,knb->ksn", picked.astype(jnp.float32), orbitals.astype(jnp.float32)).astype(jnp.bfloat16)
    twists = orbitals.shape[0]

    def add_twist(total, index):
        rows = twist_map[:, index]
        gathered = jnp.take(pairs, rows, axis=0).astype(jnp.float32)
        weight = lax.dynamic_index_in_dim(kernel, index, 0, keepdims=True).astype(jnp.float32)
        return total + gathered * weight, None

    start = jnp.zeros(pairs.shape, jnp.float32)
    summed, _ = lax.scan(add_twist, start, jnp.arange(twists, dtype=jnp.int32))
    exchange_kernel = (summed * (1.0 / twists)).astype(jnp.bfloat16)
    projector = jnp.einsum("ksn,knb->ksb", exchange_kernel.astype(jnp.float32), orbitals.astype(jnp.float32))
    return projector.astype(jnp.bfloat16)
```

```python
import functools

import jax
import jax.numpy as jnp
from jax import lax
from jax.experimental import pallas as pl
from jax.experimental.pallas import tpu as pltpu
from jax.sharding import PartitionSpec as P

X, H, C = 4, 2, 2
HALF_ROOT = 0.7071067811865476
BF, F32 = jnp.bfloat16, jnp.float32


VM = pl.BlockSpec(memory_space=pltpu.VMEM)
SM = pl.BlockSpec(memory_space=pltpu.SMEM)


def grp_perm(move):
    pairs = []
    for x in range(X):
        for h in range(H):
            for c in range(C):
                a, b, d = move(x, h, c)
                pairs.append(((x * H + h) * C + c, ((a % X) * H + b % H) * C + d % C))
    return pairs


CORE = grp_perm(lambda x, h, c: (x, h, c + 1))
ZSWAP = grp_perm(lambda x, h, c: (x, h + 1, c))
XMOVE = {d: grp_perm(lambda x, h, c, d=d: (x + d, h, c)) for d in (1, 2, 3)}


def call(kernel, outs, ins, scratch=(), flops=10**7, name=None, limit=24 << 20):
    return pl.pallas_call(
        kernel,
        out_shape=outs,
        in_specs=ins,
        out_specs=jax.tree.map(lambda _: VM, outs),
        scratch_shapes=list(scratch),
        compiler_params=pltpu.CompilerParams(vmem_limit_bytes=limit),
        cost_estimate=pl.CostEstimate(flops=flops, bytes_accessed=10**6, transcendentals=0),
        name=name,
    )


def sds(shape, dtype=BF):
    return jax.ShapeDtypeStruct(shape, dtype)


def pick_kernel(pos_ref, pts_ref, own_ref, oth_ref, *outs):
    lanes = lax.broadcasted_iota(jnp.int32, (128, 128), 1)
    pts = pts_ref[...]
    hot_own = (pts == lanes + pos_ref[0]).astype(BF)
    hot_oth = (pts == lanes + pos_ref[1]).astype(BF)
    hot = jnp.concatenate([hot_own, hot_oth], axis=1)
    for k in range(8):
        rows = jnp.concatenate([own_ref[k], oth_ref[k]], axis=0)
        got = jnp.dot(hot, rows, preferred_element_type=F32).astype(BF)
        for d in range(4):
            outs[d][k] = got[32 * d : 32 * d + 32]


def pair_kernel(pos_ref, c0, c1, c2, c3, own_ref, oth_ref, out_ref, buf):
    for k in range(8):
        left = jnp.concatenate([c0[k], c1[k], c2[k], c3[k]], axis=0)
        right = jnp.concatenate([own_ref[k], oth_ref[k]], axis=0)
        got = lax.dot_general(left, right, (((1,), (1,)), ((), ())), preferred_element_type=F32)
        for d in range(4):
            base = pl.multiple_of(pos_ref[2 + d] * 256, 256)
            buf[pl.ds(base + k, 32, stride=8), :] = got[32 * d : 32 * d + 32, :128]
            buf[pl.ds(1024 + base + k, 32, stride=8), :] = got[32 * d : 32 * d + 32, 128:]
    for t in range(16):
        out_ref[t, :, 0] = buf[64 * t : 64 * t + 64].reshape(8, 8, 128).astype(BF)
        out_ref[t, :, 1] = buf[1024 + 64 * t : 1024 + 64 * t + 64].reshape(8, 8, 128).astype(BF)


def table_kernel(map_ref, fwd_ref, inv_ref):
    e = map_ref[0, 0]

    def neg(a):
        return map_ref[e, a]

    def add(a, b):
        return map_ref[a, neg(b)]

    def dbl(a):
        return map_ref[a, neg(a)]

    def find(ok):
        return lax.while_loop(lambda l: jnp.logical_and(l < 127, jnp.logical_not(ok(l))), lambda l: l + 1, jnp.int32(0))

    def c_ok(l):
        return dbl(dbl(l)) != e

    c = find(c_ok)
    c4 = dbl(dbl(c))

    def a_ok(l):
        d = dbl(l)
        return (dbl(d) == e) & (d != e) & (d != c4)

    a = find(a_ok)
    a2 = dbl(a)
    ac = add(a2, c4)

    def b_ok(l):
        d = dbl(l)
        return (dbl(d) == e) & (d != e) & (d != c4) & (d != a2) & (d != ac)

    b = find(b_ok)
    na, nb, nc = neg(a), neg(b), neg(c)
    lane = lax.broadcasted_iota(jnp.int32, (8, 128), 1)

    def walk(n, carry):
        cur, where = carry
        where = jnp.where(lane == cur, n, where)
        cur = map_ref[cur, nc]
        cur = jnp.where(n % 8 == 7, map_ref[cur, nb], cur)
        cur = jnp.where(n % 32 == 31, map_ref[cur, na], cur)
        return cur, where

    _, where = lax.fori_loop(0, 128, walk, (e, jnp.zeros((8, 128), jnp.int32)))
    where = where[0:1]
    li, lj, ll = where // 32, (where // 8) % 4, where % 8
    f = lax.broadcasted_iota(jnp.int32, (128, 128), 0)
    fi, fj, fl = f // 32, (f // 8) % 4, f % 8
    turn = (2 * fi * li + 2 * fj * lj + fl * ll) % 8

    def parts(m):
        whole = jnp.where(m == 0, 1.0, 0.0) - jnp.where(m == 4, 1.0, 0.0)
        root = jnp.where((m == 1) | (m == 7), 1.0, 0.0) - jnp.where((m == 3) | (m == 5), 1.0, 0.0)
        return whole, root

    cw, cr = parts(turn)
    sw, sr = parts((turn + 6) % 8)
    for i, m in enumerate((cw, sw, cr, sr)):
        fwd_ref[128 * i : 128 * i + 128] = m.astype(BF)
        inv_ref[:, 128 * i : 128 * i + 128] = m.T.astype(BF)


def spectrum(fwd, cols):
    got = jnp.dot(fwd, cols, preferred_element_type=F32)
    cos = got[0:128] + HALF_ROOT * got[256:384]
    sin = got[128:256] + HALF_ROOT * got[384:512]
    return cos, sin


def kernel_spectrum(fwd_ref, own_ref, oth_ref, cos_ref, sin_ref):
    fwd = fwd_ref[...]
    for r in range(8):
        for i, ref in enumerate((own_ref, oth_ref)):
            cos, sin = spectrum(fwd, ref[r])
            cos_ref[2 * r + i] = cos * (1.0 / 128**2)
            sin_ref[2 * r + i] = sin * (1.0 / 128**2)


def conv_kernel(fwd_ref, inv_ref, kc_ref, ks_ref, p_ref, out_ref):
    fwd, inv = fwd_ref[...], inv_ref[...]
    for r in range(8):
        for i in range(2):
            cols = p_ref[:, r, i].reshape(128, 128)
            pc, ps = spectrum(fwd, cols)
            kc, ks = kc_ref[2 * r + i], ks_ref[2 * r + i]
            re = kc * pc - ks * ps
            im = kc * ps + ks * pc
            both = jnp.concatenate([re, im, HALF_ROOT * re, HALF_ROOT * im], axis=0)
            high = both.astype(BF)
            low = (both - high.astype(F32)).astype(BF)
            got = jnp.dot(inv, high, preferred_element_type=F32)
            got = got + jnp.dot(inv, low, preferred_element_type=F32)
            out_ref[:, r, i] = got.astype(BF).reshape(16, 8, 128)


def proj_kernel(pos_ref, e_ref, own_ref, oth_ref, keep_ref, s1, s2, s3, buf):
    for t in range(16):
        buf[64 * t : 64 * t + 64] = e_ref[t, :, 0].reshape(64, 128).astype(F32)
        buf[1024 + 64 * t : 1024 + 64 * t + 64] = e_ref[t, :, 1].reshape(64, 128).astype(F32)
    for k in range(8):
        rows = []
        for d in range(4):
            base = pl.multiple_of(pos_ref[6 + d] * 256, 256)
            one = buf[pl.ds(base + k, 32, stride=8), :]
            two = buf[pl.ds(1024 + base + k, 32, stride=8), :]
            rows.append(jnp.concatenate([one, two], axis=1))
        left = jnp.concatenate(rows, axis=0).astype(BF)
        right = jnp.concatenate([own_ref[k], oth_ref[k]], axis=0)
        got = jnp.dot(left, right, preferred_element_type=F32)
        keep_ref[k] = got[0:32]
        for d, ref in ((1, s1), (2, s2), (3, s3)):
            ref[k] = got[32 * d : 32 * d + 32].astype(BF)


def xsum_kernel(pos_ref, keep_ref, r1, r2, r3, kept_ref, send_ref, buf):
    buf[...] = keep_ref[...] + r1[...].astype(F32) + r2[...].astype(F32) + r3[...].astype(F32)
    h = pos_ref[10]
    kept_ref[...] = buf[:, pl.ds(pl.multiple_of(16 * h, 16), 16), :]
    send_ref[...] = buf[:, pl.ds(pl.multiple_of(16 * (1 - h), 16), 16), :].astype(BF)


def zsum_kernel(pos_ref, kept_ref, r_ref, mine_ref, send_ref, buf):
    buf[...] = kept_ref[...] + r_ref[...].astype(F32)
    c = pos_ref[11]
    mine_ref[...] = buf[:, pl.ds(pl.multiple_of(8 * c, 8), 8), :].astype(BF)
    send_ref[...] = buf[:, pl.ds(pl.multiple_of(8 * (1 - c), 8), 8), :].astype(BF)


def last_kernel(pos_ref, mine_ref, other_ref, out_ref):
    first = pos_ref[11] == 0
    mine, other = mine_ref[...].astype(F32), other_ref[...].astype(F32)
    low = jnp.where(first, mine, other)
    high = jnp.where(first, other, mine)
    out_ref[...] = jnp.concatenate([low, high], axis=1).astype(BF)


def shards(orbitals, slab_points, kernel, twist_map):
    g = lax.axis_index("grp")
    x, h, c = g // 4, (g // 2) % 2, g % 2
    oth = lax.ppermute(orbitals, "grp", CORE)
    dist = jnp.arange(4, dtype=jnp.int32)
    pos = jnp.concatenate(
        [
            jnp.stack([128 * g, 128 * (g ^ 1)]).astype(jnp.int32),
            (x - dist) % 4,
            (x + dist) % 4,
            jnp.stack([h, c]).astype(jnp.int32),
        ]
    )
    mine = lax.dynamic_index_in_dim(slab_points.reshape(4, 4, 2, 8), c, 2, keepdims=False).reshape(4, 32)
    mine = lax.dynamic_slice_in_dim(jnp.concatenate([mine, mine], axis=0), x, 4, axis=0).reshape(128, 1)
    part = call(pick_kernel, [sds((8, 32, 256))] * 4, [SM, VM, VM, VM], name="pick", flops=10**8)(
        pos, mine, orbitals, oth
    )
    halves = kernel.reshape(128, 2, 8, 128)
    k_send = lax.dynamic_index_in_dim(halves, 1 - c, 1, keepdims=False)
    k_own = lax.dynamic_index_in_dim(halves, c, 1, keepdims=False)
    k_oth = lax.ppermute(k_send, "grp", CORE)
    k_own = jnp.transpose(k_own, (1, 0, 2))
    k_oth = jnp.transpose(k_oth, (1, 0, 2))
    fwd, inv = call(table_kernel, [sds((512, 128)), sds((128, 512))], [SM], name="table", flops=10**9)(twist_map)
    kc, ks = call(kernel_spectrum, [sds((16, 128, 128), F32)] * 2, [VM] * 3, name="kspec", flops=10**9)(
        fwd, k_own, k_oth
    )

    total = part[0]
    for d in (1, 2, 3):
        total = total + lax.ppermute(part[d], "grp", XMOVE[d])
    total = total + lax.ppermute(total, "grp", ZSWAP)
    chunks = [total] + [lax.ppermute(total, "grp", XMOVE[d]) for d in (1, 2, 3)]
    pairs = call(
        pair_kernel, sds((16, 8, 2, 8, 128)), [SM] + [VM] * 6, [pltpu.VMEM((2048, 128), F32)], name="pairs", flops=10**8
    )(pos, *chunks, orbitals, oth)
    owned = lax.all_to_all(pairs, "tw", split_axis=0, concat_axis=0, tiled=True)
    exchange = call(conv_kernel, sds((16, 8, 2, 8, 128)), [VM] * 5, name="conv", flops=10**9)(fwd, inv, kc, ks, owned)
    rows = lax.all_to_all(exchange, "tw", split_axis=0, concat_axis=0, tiled=True)
    keep, s1, s2, s3 = call(
        proj_kernel,
        [sds((8, 32, 256), F32)] + [sds((8, 32, 256))] * 3,
        [SM] + [VM] * 3,
        [pltpu.VMEM((2048, 128), F32)],
        name="proj",
        flops=10**8,
    )(pos, rows, orbitals, oth)
    got = [lax.ppermute(s, "grp", XMOVE[d]) for d, s in ((1, s1), (2, s2), (3, s3))]
    kept, z_send = call(
        xsum_kernel,
        [sds((8, 16, 256), F32), sds((8, 16, 256))],
        [SM] + [VM] * 4,
        [pltpu.VMEM((8, 32, 256), F32)],
        name="xsum",
    )(pos, keep, *got)
    z_got = lax.ppermute(z_send, "grp", ZSWAP)
    done, c_send = call(
        zsum_kernel, [sds((8, 8, 256))] * 2, [SM] + [VM] * 2, [pltpu.VMEM((8, 16, 256), F32)], name="zsum"
    )(pos, kept, z_got)
    c_got = lax.ppermute(c_send, "grp", CORE)
    return call(last_kernel, sds((8, 16, 256)), [SM] + [VM] * 2, name="last")(pos, done, c_got)


def solution(mesh):
    return jax.shard_map(
        shards,
        mesh=mesh,
        in_specs=(P("tw", "grp", None), P(), P(None, "tw", "grp"), P()),
        out_specs=P("tw", "grp", None),
        check_vma=False,
    )
```

```python
import functools

import jax
import jax.numpy as jnp
from jax import lax
from jax.experimental import pallas as pl
from jax.experimental.pallas import tpu as pltpu
from jax.sharding import PartitionSpec as P

X, H, C = 4, 2, 2
HALF_ROOT = 0.7071067811865476
BF, F32 = jnp.bfloat16, jnp.float32


VM = pl.BlockSpec(memory_space=pltpu.VMEM)
SM = pl.BlockSpec(memory_space=pltpu.SMEM)


def grp_perm(move):
    pairs = []
    for x in range(X):
        for h in range(H):
            for c in range(C):
                a, b, d = move(x, h, c)
                pairs.append(((x * H + h) * C + c, ((a % X) * H + b % H) * C + d % C))
    return pairs


CORE = grp_perm(lambda x, h, c: (x, h, c + 1))
ZSWAP = grp_perm(lambda x, h, c: (x, h + 1, c))
XMOVE = {d: grp_perm(lambda x, h, c, d=d: (x ^ d, h, c)) for d in (1, 2, 3)}


def call(kernel, outs, ins, scratch=(), flops=10**7, name=None, limit=24 << 20):
    return pl.pallas_call(
        kernel,
        out_shape=outs,
        in_specs=ins,
        out_specs=jax.tree.map(lambda _: VM, outs),
        scratch_shapes=list(scratch),
        compiler_params=pltpu.CompilerParams(vmem_limit_bytes=limit),
        cost_estimate=pl.CostEstimate(flops=flops, bytes_accessed=10**6, transcendentals=0),
        name=name,
    )


def sds(shape, dtype=BF):
    return jax.ShapeDtypeStruct(shape, dtype)


def hot_rows(pos_ref, pts_ref, base, hot):
    sub = lax.broadcasted_iota(jnp.int32, (128, 128), 0) + base
    for a in range(2):
        hot[128 * a : 128 * a + 128] = (pts_ref[a : a + 1] == sub).astype(F32).T
    rows = []
    for d in range(4):
        for w in range(4):
            start = pl.multiple_of(64 * pos_ref[2 + d] + 16 * w + 8 * pos_ref[7], 8)
            rows.append(hot[pl.ds(start, 8)])
    return jnp.concatenate(rows, axis=0).astype(BF)


def pick_own_kernel(pos_ref, pts_ref, own_ref, out_ref, hot):
    rows = hot_rows(pos_ref, pts_ref, pos_ref[0], hot)
    for k in range(8):
        out_ref[k] = jnp.dot(rows, own_ref[k], preferred_element_type=F32).astype(BF)


def pick_kernel(pos_ref, pts_ref, first_ref, oth_ref, o0, o1, o2, o3, hot):
    rows = hot_rows(pos_ref, pts_ref, pos_ref[1], hot)
    for k in range(8):
        got = jnp.dot(rows, oth_ref[k], preferred_element_type=F32)
        got = (got + first_ref[k].astype(F32)).astype(BF)
        for d, ref in enumerate((o0, o1, o2, o3)):
            ref[k] = got[32 * d : 32 * d + 32]


def pair_kernel(pos_ref, c0, c1, c2, c3, own_ref, oth_ref, out_ref, buf):
    for k in range(8):
        left = jnp.concatenate([c0[k], c1[k], c2[k], c3[k]], axis=0)
        right = jnp.concatenate([own_ref[k], oth_ref[k]], axis=0)
        got = lax.dot_general(left, right, (((1,), (1,)), ((), ())), preferred_element_type=F32)
        for d in range(4):
            base = pl.multiple_of(pos_ref[2 + d] * 256, 256)
            buf[pl.ds(base + k, 32, stride=8), :] = got[32 * d : 32 * d + 32, :128]
            buf[pl.ds(1024 + base + k, 32, stride=8), :] = got[32 * d : 32 * d + 32, 128:]
    for t in range(16):
        out_ref[t, :, 0] = buf[64 * t : 64 * t + 64].reshape(8, 8, 128).astype(BF)
        out_ref[t, :, 1] = buf[1024 + 64 * t : 1024 + 64 * t + 64].reshape(8, 8, 128).astype(BF)


def table_kernel(map_ref, fwd_ref, inv_ref):
    e = map_ref[0, 0]

    def neg(a):
        return map_ref[e, a]

    def add(a, b):
        return map_ref[a, neg(b)]

    def dbl(a):
        return map_ref[a, neg(a)]

    def find(ok):
        return lax.while_loop(lambda l: jnp.logical_and(l < 127, jnp.logical_not(ok(l))), lambda l: l + 1, jnp.int32(0))

    def c_ok(l):
        return dbl(dbl(l)) != e

    c = find(c_ok)
    c4 = dbl(dbl(c))

    def a_ok(l):
        d = dbl(l)
        return (dbl(d) == e) & (d != e) & (d != c4)

    a = find(a_ok)
    a2 = dbl(a)
    ac = add(a2, c4)

    def b_ok(l):
        d = dbl(l)
        return (dbl(d) == e) & (d != e) & (d != c4) & (d != a2) & (d != ac)

    b = find(b_ok)
    na, nb, nc = neg(a), neg(b), neg(c)
    lane = lax.broadcasted_iota(jnp.int32, (8, 128), 1)

    def walk(n, carry):
        cur, where = carry
        where = jnp.where(lane == cur, n, where)
        cur = map_ref[cur, nc]
        cur = jnp.where(n % 8 == 7, map_ref[cur, nb], cur)
        cur = jnp.where(n % 32 == 31, map_ref[cur, na], cur)
        return cur, where

    _, where = lax.fori_loop(0, 128, walk, (e, jnp.zeros((8, 128), jnp.int32)))
    where = where[0:1]
    li, lj, ll = where // 32, (where // 8) % 4, where % 8
    row = lax.broadcasted_iota(jnp.int32, (80, 128), 0)
    fi, fj = (row // 4) % 4, row % 4
    fl = jnp.where(row < 48, 2 * (row // 16), 2 * (row // 16) - 5)
    turn = (2 * fi * li + 2 * fj * lj + fl * ll) % 8

    def parts(m):
        whole = jnp.where(m == 0, 1.0, 0.0) - jnp.where(m == 4, 1.0, 0.0)
        root = jnp.where((m == 1) | (m == 7), 1.0, 0.0) - jnp.where((m == 3) | (m == 5), 1.0, 0.0)
        return whole, root[48:80]

    cw, cr = parts(turn)
    sw, sr = parts((turn + 6) % 8)
    whole = jnp.concatenate([cw, sw, cr, sr, jnp.zeros((32, 128), F32)], axis=0)
    fwd_ref[...] = whole[0:224].astype(BF)
    inv_ref[...] = whole.T.astype(BF)


def with_root(got, root):
    return jnp.concatenate([got[0:48], got[48:80] + HALF_ROOT * root], axis=0)


def spectrum(fwd, cols):
    got = jnp.dot(fwd, cols, preferred_element_type=F32)
    return with_root(got[0:80], got[160:192]), with_root(got[80:160], got[192:224])


def kernel_spectrum(fwd_ref, own_ref, oth_ref, cos_ref, sin_ref):
    fwd = fwd_ref[...]
    row = lax.broadcasted_iota(jnp.int32, (80, 256), 0)
    alone = (row < 16) | ((row >= 32) & (row < 48))
    scale = jnp.where(alone, 1.0 / 128**2, 2.0 / 128**2)
    for r in range(8):
        cos, sin = spectrum(fwd, jnp.concatenate([own_ref[r], oth_ref[r]], axis=1))
        cos_ref[r] = cos * scale
        sin_ref[r] = sin * scale


def conv_kernel(fwd_ref, inv_ref, kc_ref, ks_ref, p_ref, out_ref):
    fwd, inv = fwd_ref[...], inv_ref[...]
    for r in range(8):
        cols = jnp.concatenate([p_ref[:, r, 0].reshape(128, 128), p_ref[:, r, 1].reshape(128, 128)], axis=1)
        pc, ps = spectrum(fwd, cols)
        kc, ks = kc_ref[r], ks_ref[r]
        re = kc * pc - ks * ps
        im = kc * ps + ks * pc
        both = [re, im, HALF_ROOT * re[48:80], HALF_ROOT * im[48:80], jnp.zeros((32, 256), F32)]
        both = jnp.concatenate(both, axis=0)
        high = both.astype(BF)
        low = (both - high.astype(F32)).astype(BF)
        got = jnp.dot(inv, high, preferred_element_type=F32)
        got = (got + jnp.dot(inv, low, preferred_element_type=F32)).astype(BF)
        out_ref[:, r, 0] = got[:, :128].reshape(16, 8, 128)
        out_ref[:, r, 1] = got[:, 128:].reshape(16, 8, 128)


def proj_kernel(pos_ref, e_ref, own_ref, oth_ref, keep_ref, s1, s2, s3, buf):
    for t in range(16):
        buf[64 * t : 64 * t + 64] = e_ref[t, :, 0].reshape(64, 128).astype(F32)
        buf[1024 + 64 * t : 1024 + 64 * t + 64] = e_ref[t, :, 1].reshape(64, 128).astype(F32)
    for k in range(8):
        rows = []
        for d in range(4):
            base = pl.multiple_of(pos_ref[2 + d] * 256, 256)
            one = buf[pl.ds(base + k, 32, stride=8), :]
            two = buf[pl.ds(1024 + base + k, 32, stride=8), :]
            rows.append(jnp.concatenate([one, two], axis=1))
        left = jnp.concatenate(rows, axis=0).astype(BF)
        right = jnp.concatenate([own_ref[k], oth_ref[k]], axis=0)
        got = jnp.dot(left, right, preferred_element_type=F32)
        keep_ref[k] = got[0:32]
        for d, ref in ((1, s1), (2, s2), (3, s3)):
            ref[k] = got[32 * d : 32 * d + 32].astype(BF)


def xsum_kernel(pos_ref, keep_ref, r1, r2, r3, kept_ref, send_ref, buf):
    buf[...] = keep_ref[...] + r1[...].astype(F32) + r2[...].astype(F32) + r3[...].astype(F32)
    h = pos_ref[6]
    kept_ref[...] = buf[:, pl.ds(pl.multiple_of(16 * h, 16), 16), :]
    send_ref[...] = buf[:, pl.ds(pl.multiple_of(16 * (1 - h), 16), 16), :].astype(BF)


def zsum_kernel(pos_ref, kept_ref, r_ref, mine_ref, send_ref, buf):
    buf[...] = kept_ref[...] + r_ref[...].astype(F32)
    c = pos_ref[7]
    mine_ref[...] = buf[:, pl.ds(pl.multiple_of(8 * c, 8), 8), :].astype(BF)
    send_ref[...] = buf[:, pl.ds(pl.multiple_of(8 * (1 - c), 8), 8), :].astype(BF)


def last_kernel(pos_ref, mine_ref, other_ref, out_ref):
    first = pos_ref[7] == 0
    mine, other = mine_ref[...].astype(F32), other_ref[...].astype(F32)
    low = jnp.where(first, mine, other)
    high = jnp.where(first, other, mine)
    out_ref[...] = jnp.concatenate([low, high], axis=1).astype(BF)


def shards(orbitals, slab_points, kernel, twist_map):
    g = lax.axis_index("grp")
    x, h, c = g // 4, (g // 2) % 2, g % 2
    oth = lax.ppermute(orbitals, "grp", CORE)
    pos = jnp.stack([128 * g, 128 * (g ^ 1), x, x ^ 1, x ^ 2, x ^ 3, h, c]).astype(jnp.int32)
    points = slab_points.reshape(2, 128)
    hot = [pltpu.VMEM((256, 128), F32)]
    first = call(pick_own_kernel, sds((8, 128, 256)), [SM, VM, VM], hot, name="pick_own", flops=10**8)(
        pos, points, orbitals
    )
    part = call(pick_kernel, [sds((8, 32, 256))] * 4, [SM, VM, VM, VM], hot, name="pick", flops=10**8)(
        pos, points, first, oth
    )
    halves = kernel.reshape(128, 2, 8, 128)
    k_send = lax.dynamic_index_in_dim(halves, 1 - c, 1, keepdims=False)
    k_own = lax.dynamic_index_in_dim(halves, c, 1, keepdims=False)
    k_oth = lax.ppermute(k_send, "grp", CORE)
    k_own = jnp.transpose(k_own, (1, 0, 2))
    k_oth = jnp.transpose(k_oth, (1, 0, 2))
    fwd, inv = call(table_kernel, [sds((224, 128)), sds((128, 256))], [SM], name="table", flops=10**9)(twist_map)

    got = [lax.ppermute(part[d], "grp", XMOVE[d]) for d in (1, 2, 3)]
    *got, fwd, inv, k_own, k_oth = lax.optimization_barrier((*got, fwd, inv, k_own, k_oth))
    total = part[0] + got[0] + got[1] + got[2]
    kc, ks = call(kernel_spectrum, [sds((8, 80, 256), F32)] * 2, [VM] * 3, name="kspec", flops=10**9)(
        fwd, k_own, k_oth
    )
    from_z = lax.ppermute(total, "grp", ZSWAP)
    from_z, kc, ks = lax.optimization_barrier((from_z, kc, ks))
    total = total + from_z
    chunks = [total] + [lax.ppermute(total, "grp", XMOVE[d]) for d in (1, 2, 3)]
    pairs = call(
        pair_kernel, sds((16, 8, 2, 8, 128)), [SM] + [VM] * 6, [pltpu.VMEM((2048, 128), F32)], name="pairs", flops=10**8
    )(pos, *chunks, orbitals, oth)
    owned = lax.all_to_all(pairs, "tw", split_axis=0, concat_axis=0, tiled=True)
    exchange = call(conv_kernel, sds((16, 8, 2, 8, 128)), [VM] * 5, name="conv", flops=10**9)(fwd, inv, kc, ks, owned)
    rows = lax.all_to_all(exchange, "tw", split_axis=0, concat_axis=0, tiled=True)
    keep, s1, s2, s3 = call(
        proj_kernel,
        [sds((8, 32, 256), F32)] + [sds((8, 32, 256))] * 3,
        [SM] + [VM] * 3,
        [pltpu.VMEM((2048, 128), F32)],
        name="proj",
        flops=10**8,
    )(pos, rows, orbitals, oth)
    got = [lax.ppermute(s, "grp", XMOVE[d]) for d, s in ((1, s1), (2, s2), (3, s3))]
    kept, z_send = call(
        xsum_kernel,
        [sds((8, 16, 256), F32), sds((8, 16, 256))],
        [SM] + [VM] * 4,
        [pltpu.VMEM((8, 32, 256), F32)],
        name="xsum",
    )(pos, keep, *got)
    z_got = lax.ppermute(z_send, "grp", ZSWAP)
    done, c_send = call(
        zsum_kernel, [sds((8, 8, 256))] * 2, [SM] + [VM] * 2, [pltpu.VMEM((8, 16, 256), F32)], name="zsum"
    )(pos, kept, z_got)
    c_got = lax.ppermute(c_send, "grp", CORE)
    return call(last_kernel, sds((8, 16, 256)), [SM] + [VM] * 2, name="last")(pos, done, c_got)


def solution(mesh):
    return jax.shard_map(
        shards,
        mesh=mesh,
        in_specs=(P("tw", "grp", None), P(), P(None, "tw", "grp"), P()),
        out_specs=P("tw", "grp", None),
        check_vma=False,
    )
```

```python
import functools

import jax
import jax.numpy as jnp
from jax import lax
from jax.experimental import pallas as pl
from jax.experimental.pallas import tpu as pltpu
from jax.sharding import PartitionSpec as P

X, H, C, Y, W = 4, 2, 2, 4, 4
HALF_ROOT = 0.7071067811865476
BF, F32 = jnp.bfloat16, jnp.float32


VM = pl.BlockSpec(memory_space=pltpu.VMEM)
SM = pl.BlockSpec(memory_space=pltpu.SMEM)


def grp_perm(move):
    pairs = []
    for x in range(X):
        for h in range(H):
            for c in range(C):
                a, b, d = move(x, h, c)
                pairs.append(((x * H + h) * C + c, ((a % X) * H + b % H) * C + d % C))
    return pairs


def all_perm(move):
    pairs = []
    for x in range(X):
        for q in range(H * C):
            for y in range(Y):
                for w in range(W):
                    a, b = move(x, y)
                    pairs.append(((x * H * C + q) * Y * W + y * W + w, (a * H * C + q) * Y * W + b * W + w))
    return pairs


CORE = grp_perm(lambda x, h, c: (x, h, c + 1))
ZSWAP = grp_perm(lambda x, h, c: (x, h + 1, c))
XMOVE = {d: grp_perm(lambda x, h, c, d=d: (x ^ d, h, c)) for d in (1, 2, 3)}
KMOVE = [all_perm(lambda x, y, e=e: (y, x ^ e)) for e in range(4)]

BASE, PX, PY, PH, PC = 0, 1, 5, 9, 10


def call(kernel, outs, ins, scratch=(), flops=10**7, name=None, limit=24 << 20):
    return pl.pallas_call(
        kernel,
        out_shape=outs,
        in_specs=ins,
        out_specs=jax.tree.map(lambda _: VM, outs),
        scratch_shapes=list(scratch),
        compiler_params=pltpu.CompilerParams(vmem_limit_bytes=limit),
        cost_estimate=pl.CostEstimate(flops=flops, bytes_accessed=10**6, transcendentals=0),
        name=name,
    )


def sds(shape, dtype=BF):
    return jax.ShapeDtypeStruct(shape, dtype)


def pick_kernel(pos_ref, pts_ref, own_ref, k0, k1, k2, k3, send_ref, hot):
    sub = lax.broadcasted_iota(jnp.int32, (128, 128), 0) + pos_ref[BASE]
    for a in range(2):
        hot[128 * a : 128 * a + 128] = (pts_ref[a : a + 1] == sub).astype(F32).T
    halves = []
    for half in (pos_ref[PC], 1 - pos_ref[PC]):
        for d in range(4):
            halves.append(hot[pl.ds(pl.multiple_of(64 * pos_ref[PX + d] + 32 * half, 32), 32)])
    rows = jnp.concatenate(halves, axis=0).astype(BF)
    for k in range(8):
        got = jnp.dot(rows, own_ref[k], preferred_element_type=F32).astype(BF)
        for d, ref in enumerate((k0, k1, k2, k3)):
            ref[k] = got[32 * d : 32 * d + 32]
        send_ref[k] = got[128:256]


def points_of(k, own, b1, lo, hi, b3):
    two = lo[k] if k < 4 else hi[k - 4]
    return jnp.concatenate([own[k], b1[k], two, b3[k]], axis=0)


def pair_kernel(pos_ref, mine, theirs, own, b1, lo, hi, b3, out_ref, buf):
    c = pos_ref[PC]
    for k in range(8):
        left = jnp.concatenate([mine[k], theirs[k]], axis=0)
        right = points_of(k, own, b1, lo, hi, b3)
        got = lax.dot_general(left, right, (((1,), (1,)), ((), ())), preferred_element_type=F32)
        for j in range(4):
            for i, half in enumerate((c, 1 - c)):
                base = pl.multiple_of(pos_ref[PX + j] * 512 + half * 256, 256)
                buf[pl.ds(base + k, 32, stride=8), :] = got[32 * i : 32 * i + 32, 128 * j : 128 * j + 128]
    for x in range(4):
        for w in range(4):
            for y in range(4):
                row = 512 * x + 128 * w + 32 * y
                out_ref[4 * y + w, :, x] = buf[row : row + 32].reshape(4, 8, 128).astype(BF)


def table_kernel(map_ref, fwd_ref, inv_ref):
    e = map_ref[0, 0]

    def neg(a):
        return map_ref[e, a]

    def add(a, b):
        return map_ref[a, neg(b)]

    def dbl(a):
        return map_ref[a, neg(a)]

    def find(ok):
        return lax.while_loop(lambda l: jnp.logical_and(l < 127, jnp.logical_not(ok(l))), lambda l: l + 1, jnp.int32(0))

    def c_ok(l):
        return dbl(dbl(l)) != e

    c = find(c_ok)
    c4 = dbl(dbl(c))

    def a_ok(l):
        d = dbl(l)
        return (dbl(d) == e) & (d != e) & (d != c4)

    a = find(a_ok)
    a2 = dbl(a)
    ac = add(a2, c4)

    def b_ok(l):
        d = dbl(l)
        return (dbl(d) == e) & (d != e) & (d != c4) & (d != a2) & (d != ac)

    b = find(b_ok)
    na, nb, nc = neg(a), neg(b), neg(c)
    lane = lax.broadcasted_iota(jnp.int32, (8, 128), 1)

    def walk(n, carry):
        cur, where = carry
        where = jnp.where(lane == cur, n, where)
        cur = map_ref[cur, nc]
        cur = jnp.where(n % 8 == 7, map_ref[cur, nb], cur)
        cur = jnp.where(n % 32 == 31, map_ref[cur, na], cur)
        return cur, where

    _, where = lax.fori_loop(0, 128, walk, (e, jnp.zeros((8, 128), jnp.int32)))
    where = where[0:1]
    li, lj, ll = where // 32, (where // 8) % 4, where % 8
    row = lax.broadcasted_iota(jnp.int32, (80, 128), 0)
    fi, fj = (row // 4) % 4, row % 4
    fl = jnp.where(row < 48, 2 * (row // 16), 2 * (row // 16) - 5)
    turn = (2 * fi * li + 2 * fj * lj + fl * ll) % 8

    def parts(m):
        whole = jnp.where(m == 0, 1.0, 0.0) - jnp.where(m == 4, 1.0, 0.0)
        root = jnp.where((m == 1) | (m == 7), 1.0, 0.0) - jnp.where((m == 3) | (m == 5), 1.0, 0.0)
        return whole, root[48:80]

    cw, cr = parts(turn)
    sw, sr = parts((turn + 6) % 8)
    whole = jnp.concatenate([cw, sw, cr, sr, jnp.zeros((32, 128), F32)], axis=0)
    fwd_ref[...] = whole[0:224].astype(BF)
    inv_ref[...] = whole.T.astype(BF)


def with_root(got, root):
    return jnp.concatenate([got[0:48], got[48:80] + HALF_ROOT * root], axis=0)


def spectrum(fwd, cols):
    got = jnp.dot(fwd, cols, preferred_element_type=F32)
    return with_root(got[0:80], got[160:192]), with_root(got[80:160], got[192:224])


def split_kernel(pos_ref, k_ref, o0, o1, o2, o3, buf):
    buf[...] = k_ref[...].reshape(2048, 128).astype(F32)
    for e, ref in enumerate((o0, o1, o2, o3)):
        for r in range(4):
            ref[r] = buf[pl.ds(4 * pos_ref[PX + e] + r, 128, stride=16), :].astype(BF)


def kernel_spectrum(pos_ref, fwd_ref, p0, p1, p2, p3, cos_ref, sin_ref):
    fwd = fwd_ref[...]
    row = lax.broadcasted_iota(jnp.int32, (80, 256), 0)
    alone = (row < 16) | ((row >= 32) & (row < 48))
    scale = jnp.where(alone, 1.0 / 128**2, 2.0 / 128**2)
    for e, (one, two) in ((0, (p0, p1)), (2, (p2, p3))):
        for r in range(4):
            cos, sin = spectrum(fwd, jnp.concatenate([one[r], two[r]], axis=1))
            cos, sin = cos * scale, sin * scale
            for i in range(2):
                x = pos_ref[PY + e + i]
                cos_ref[x, r] = cos[:, 128 * i : 128 * i + 128]
                sin_ref[x, r] = sin[:, 128 * i : 128 * i + 128]


def conv_kernel(fwd_ref, inv_ref, kc_ref, ks_ref, p_ref, out_ref):
    fwd, inv = fwd_ref[...], inv_ref[...]
    for r in range(4):
        for x in (0, 2):
            cols = jnp.concatenate([p_ref[:, r, x].reshape(128, 128), p_ref[:, r, x + 1].reshape(128, 128)], axis=1)
            pc, ps = spectrum(fwd, cols)
            kc = jnp.concatenate([kc_ref[x, r], kc_ref[x + 1, r]], axis=1)
            ks = jnp.concatenate([ks_ref[x, r], ks_ref[x + 1, r]], axis=1)
            re = kc * pc - ks * ps
            im = kc * ps + ks * pc
            both = [re, im, HALF_ROOT * re[48:80], HALF_ROOT * im[48:80], jnp.zeros((32, 256), F32)]
            both = jnp.concatenate(both, axis=0)
            high = both.astype(BF)
            low = (both - high.astype(F32)).astype(BF)
            got = jnp.dot(inv, high, preferred_element_type=F32)
            got = (got + jnp.dot(inv, low, preferred_element_type=F32)).astype(BF)
            out_ref[:, r, x] = got[:, :128].reshape(16, 8, 128)
            out_ref[:, r, x + 1] = got[:, 128:].reshape(16, 8, 128)


def proj_kernel(pos_ref, e_ref, own, b1, lo, hi, b3, keep_ref, send_ref, buf, res):
    for x in range(4):
        for w in range(4):
            for y in range(4):
                row = 512 * x + 128 * w + 32 * y
                buf[row : row + 32] = e_ref[4 * y + w, :, x].reshape(32, 128).astype(F32)
    c = pos_ref[PC]
    for k in range(8):
        parts = [buf[pl.ds(pl.multiple_of(pos_ref[PX + j] * 512, 512) + k, 64, stride=8), :] for j in range(4)]
        left = jnp.concatenate(parts, axis=1).astype(BF)
        got = jnp.dot(left, points_of(k, own, b1, lo, hi, b3), preferred_element_type=F32)
        res[k] = got.reshape(4, 16, 256)
        for h in range(2):
            keep_ref[k, h] = res[k, 2 * h + c]
            send_ref[k, h] = res[k, 2 * h + 1 - c].astype(BF)


def shards(orbitals, slab_points, kernel, twist_map):
    g, t = lax.axis_index("grp"), lax.axis_index("tw")
    x, h, c = g >> 2, (g >> 1) & 1, g & 1
    y = t >> 2
    pos = jnp.stack([128 * g, x, x ^ 1, x ^ 2, x ^ 3, y, y ^ 1, y ^ 2, y ^ 3, h, c]).astype(jnp.int32)

    b1 = lax.ppermute(orbitals, "grp", XMOVE[1])
    b3 = lax.ppermute(orbitals, "grp", XMOVE[3])

    *part, send = call(
        pick_kernel,
        [sds((8, 32, 256))] * 4 + [sds((8, 128, 256))],
        [SM, VM, VM],
        [pltpu.VMEM((256, 128), F32)],
        name="pick",
        flops=10**8,
    )(pos, slab_points.reshape(2, 128), orbitals)
    recv = lax.ppermute(send, "grp", CORE)
    part = [p + recv[:, 32 * d : 32 * d + 32] for d, p in enumerate(part)]
    got = [lax.ppermute(part[d], "grp", XMOVE[d]) for d in (1, 2, 3)]
    fwd, inv = call(table_kernel, [sds((224, 128)), sds((128, 256))], [SM], name="table", flops=10**9)(twist_map)
    pieces = call(
        split_kernel, [sds((4, 128, 128))] * 4, [SM, VM], [pltpu.VMEM((2048, 128), F32)], name="split", flops=10**9
    )(pos, kernel)
    *got, fwd, inv, p0, p1, p2, p3, b1, b3 = lax.optimization_barrier((*got, fwd, inv, *pieces, b1, b3))
    pieces = (p0, p1, p2, p3)
    total = part[0] + got[0] + got[1] + got[2]
    from_z = lax.ppermute(total, "grp", ZSWAP)
    lo = lax.ppermute(b3[:4], "grp", XMOVE[1])
    hi = lax.ppermute(b1[4:], "grp", XMOVE[3])
    pieces = [lax.ppermute(p, ("grp", "tw"), KMOVE[e]) for e, p in enumerate(pieces)]
    total = total + from_z
    theirs = lax.ppermute(total, "grp", CORE)
    kc, ks = call(
        kernel_spectrum, [sds((4, 4, 80, 128), F32)] * 2, [SM] + [VM] * 5, name="kspec", flops=10**9
    )(pos, fwd, *pieces)
    blocks = (orbitals, b1, lo, hi, b3)
    pairs = call(
        pair_kernel, sds((16, 4, 4, 8, 128)), [SM] + [VM] * 7, [pltpu.VMEM((2048, 128), F32)], name="pairs", flops=10**8
    )(pos, total, theirs, *blocks)
    pairs, kc, ks = lax.optimization_barrier((pairs, kc, ks))
    owned = lax.all_to_all(pairs, "tw", split_axis=0, concat_axis=0, tiled=True)
    exchange = call(conv_kernel, sds((16, 4, 4, 8, 128)), [VM] * 5, name="conv", flops=10**9)(fwd, inv, kc, ks, owned)
    rows = lax.all_to_all(exchange, "tw", split_axis=0, concat_axis=0, tiled=True)
    keep, send = call(
        proj_kernel,
        [sds((8, 2, 16, 256), F32), sds((8, 2, 16, 256))],
        [SM] + [VM] * 6,
        [pltpu.VMEM((2048, 128), F32), pltpu.VMEM((8, 4, 16, 256), F32)],
        name="proj",
        flops=10**8,
    )(pos, rows, *blocks)
    both = keep + lax.ppermute(send, "grp", CORE).astype(F32)
    z_send = lax.dynamic_index_in_dim(both, 1 - h, 1, keepdims=False).astype(BF)
    kept = lax.dynamic_index_in_dim(both, h, 1, keepdims=False)
    return (kept + lax.ppermute(z_send, "grp", ZSWAP).astype(F32)).astype(BF)


def solution(mesh):
    return jax.shard_map(
        shards,
        mesh=mesh,
        in_specs=(P("tw", "grp", None), P(), P(None, "tw", "grp"), P()),
        out_specs=P("tw", "grp", None),
        check_vma=False,
    )
```

```python
import jax
import jax.numpy as jnp
from jax import lax
from jax.experimental import pallas as pl
from jax.experimental.pallas import tpu as pltpu
from jax.sharding import PartitionSpec as P


X, H, C, Y, W = 4, 2, 2, 4, 4
HALF_ROOT = 0.7071067811865476
BF, F32 = jnp.bfloat16, jnp.float32


VM = pl.BlockSpec(memory_space=pltpu.VMEM)
SM = pl.BlockSpec(memory_space=pltpu.SMEM)


def grp_perm(move):
    pairs = []
    for x in range(X):
        for h in range(H):
            for c in range(C):
                a, b, d = move(x, h, c)
                pairs.append(((x * H + h) * C + c, ((a % X) * H + b % H) * C + d % C))
    return pairs


CORE = grp_perm(lambda x, h, c: (x, h, c + 1))
ZSWAP = grp_perm(lambda x, h, c: (x, h + 1, c))
XMOVE = {d: grp_perm(lambda x, h, c, d=d: (x ^ d, h, c)) for d in (1, 2, 3)}
YMOVE = {e: [(t, t ^ (e * W)) for t in range(Y * W)] for e in (1, 2, 3)}

BASE, PX, PY, PC = 0, 1, 5, 10


def call(kernel, outs, ins, scratch=(), flops=10**7, limit=24 << 20):
    return pl.pallas_call(
        kernel,
        out_shape=outs,
        in_specs=ins,
        out_specs=jax.tree.map(lambda _: VM, outs),
        scratch_shapes=list(scratch),
        compiler_params=pltpu.CompilerParams(vmem_limit_bytes=limit),
        cost_estimate=pl.CostEstimate(flops=flops, bytes_accessed=10**6, transcendentals=0),
    )


def sds(shape, dtype=BF):
    return jax.ShapeDtypeStruct(shape, dtype)


def pick_kernel(pos_ref, pts_ref, own_ref, k0, k1, k2, k3, send_ref, copy_ref, hot):
    sub = lax.broadcasted_iota(jnp.int32, (128, 128), 0) + pos_ref[BASE]
    for a in range(2):
        hot[128 * a : 128 * a + 128] = (pts_ref[a : a + 1] == sub).astype(F32).T
    halves = []
    for half in (pos_ref[PC], 1 - pos_ref[PC]):
        for d in range(4):
            halves.append(hot[pl.ds(pl.multiple_of(64 * pos_ref[PX + d] + 32 * half, 32), 32)])
    rows = jnp.concatenate(halves, axis=0).astype(BF)
    for k in range(8):
        got = jnp.dot(rows, own_ref[k], preferred_element_type=F32).astype(BF)
        for d, ref in enumerate((k0, k1, k2, k3)):
            ref[k] = got[32 * d : 32 * d + 32]
        send_ref[k] = got[128:256]
    copy_ref[...] = own_ref[...]


def points_of(k, own, b1, lo, hi, b3):
    two = lo[k] if k < 4 else hi[k - 4]
    return jnp.concatenate([own[k], b1[k], two, b3[k]], axis=0)


def pair_kernel(pos_ref, mine, theirs, own, b1, lo, hi, b3, out_ref, buf):
    c = pos_ref[PC]
    for k in range(8):
        left = jnp.concatenate([mine[k], theirs[k]], axis=0)
        right = points_of(k, own, b1, lo, hi, b3)
        got = lax.dot_general(left, right, (((1,), (1,)), ((), ())), preferred_element_type=F32)
        for j in range(4):
            for i, half in enumerate((c, 1 - c)):
                base = pl.multiple_of(pos_ref[PX + j] * 512 + half * 256, 256)
                buf[pl.ds(base + k, 32, stride=8), :] = got[32 * i : 32 * i + 32, 128 * j : 128 * j + 128]
    for x in range(4):
        for w in range(4):
            for y in range(4):
                row = 512 * x + 128 * w + 32 * y
                out_ref[4 * y + w, :, x] = buf[row : row + 32].reshape(4, 8, 128).astype(BF)


def table_kernel(map_ref, fwd_ref, inv_ref):
    e = map_ref[0, 0]

    def neg(a):
        return map_ref[e, a]

    def add(a, b):
        return map_ref[a, neg(b)]

    def dbl(a):
        return map_ref[a, neg(a)]

    def find(ok):
        return lax.while_loop(lambda l: jnp.logical_and(l < 127, jnp.logical_not(ok(l))), lambda l: l + 1, jnp.int32(0))

    def c_ok(l):
        return dbl(dbl(l)) != e

    c = find(c_ok)
    c4 = dbl(dbl(c))

    def a_ok(l):
        d = dbl(l)
        return (dbl(d) == e) & (d != e) & (d != c4)

    a = find(a_ok)
    a2 = dbl(a)
    ac = add(a2, c4)

    def b_ok(l):
        d = dbl(l)
        return (dbl(d) == e) & (d != e) & (d != c4) & (d != a2) & (d != ac)

    b = find(b_ok)
    na, nb, nc = neg(a), neg(b), neg(c)
    lane = lax.broadcasted_iota(jnp.int32, (8, 128), 1)

    def walk(n, carry):
        cur, where = carry
        where = jnp.where(lane == cur, n, where)
        cur = map_ref[cur, nc]
        cur = jnp.where(n % 8 == 7, map_ref[cur, nb], cur)
        cur = jnp.where(n % 32 == 31, map_ref[cur, na], cur)
        return cur, where

    _, where = lax.fori_loop(0, 128, walk, (e, jnp.zeros((8, 128), jnp.int32)))
    where = where[0:1]
    li, lj, ll = where // 32, (where // 8) % 4, where % 8
    row = lax.broadcasted_iota(jnp.int32, (80, 128), 0)
    fi, fj = (row // 4) % 4, row % 4
    fl = jnp.where(row < 48, 2 * (row // 16), 2 * (row // 16) - 5)
    turn = (2 * fi * li + 2 * fj * lj + fl * ll) % 8

    def parts(m):
        whole = jnp.where(m == 0, 1.0, 0.0) - jnp.where(m == 4, 1.0, 0.0)
        root = jnp.where((m == 1) | (m == 7), 1.0, 0.0) - jnp.where((m == 3) | (m == 5), 1.0, 0.0)
        return whole, root[48:80]

    cw, cr = parts(turn)
    sw, sr = parts((turn + 6) % 8)
    whole = jnp.concatenate([cw, sw, cr, sr, jnp.zeros((32, 128), F32)], axis=0)
    fwd_ref[...] = whole[0:224].astype(BF)
    inv_ref[...] = whole.T.astype(BF)


def with_root(got, root):
    return jnp.concatenate([got[0:48], got[48:80] + HALF_ROOT * root], axis=0)


def spectrum(fwd, cols):
    got = jnp.dot(fwd, cols, preferred_element_type=F32)
    return with_root(got[0:80], got[160:192]), with_root(got[80:160], got[192:224])


def split_kernel(pos_ref, k_ref, o0, o1, o2, o3, buf):
    buf[...] = k_ref[...].reshape(2048, 128).astype(F32)
    for e, ref in enumerate((o0, o1, o2, o3)):
        for r in range(4):
            ref[r] = buf[pl.ds(4 * pos_ref[PY + e] + r, 128, stride=16), :].astype(BF)


def turn_kernel(pos_ref, p0, p1, p2, p3, o0, o1, o2, o3, buf):
    for e, ref in enumerate((p0, p1, p2, p3)):
        buf[e] = ref[...]
    y = pos_ref[PY]
    for d, ref in enumerate((o0, o1, o2, o3)):
        ref[...] = buf[y ^ pos_ref[PX + d]]


def kernel_spectrum(pos_ref, fwd_ref, p0, p1, p2, p3, cos_ref, sin_ref):
    fwd = fwd_ref[...]
    row = lax.broadcasted_iota(jnp.int32, (80, 256), 0)
    alone = (row < 16) | ((row >= 32) & (row < 48))
    scale = jnp.where(alone, 1.0 / 128**2, 2.0 / 128**2)
    for e, (one, two) in ((0, (p0, p1)), (2, (p2, p3))):
        for r in range(4):
            cos, sin = spectrum(fwd, jnp.concatenate([one[r], two[r]], axis=1))
            cos, sin = cos * scale, sin * scale
            for i in range(2):
                x = pos_ref[PX + e + i]
                cos_ref[x, r] = cos[:, 128 * i : 128 * i + 128]
                sin_ref[x, r] = sin[:, 128 * i : 128 * i + 128]


def conv_kernel(fwd_ref, inv_ref, kc_ref, ks_ref, p_ref, out_ref):
    fwd, inv = fwd_ref[...], inv_ref[...]
    for r in range(4):
        for x in (0, 2):
            cols = jnp.concatenate([p_ref[:, r, x].reshape(128, 128), p_ref[:, r, x + 1].reshape(128, 128)], axis=1)
            pc, ps = spectrum(fwd, cols)
            kc = jnp.concatenate([kc_ref[x, r], kc_ref[x + 1, r]], axis=1)
            ks = jnp.concatenate([ks_ref[x, r], ks_ref[x + 1, r]], axis=1)
            re = kc * pc - ks * ps
            im = kc * ps + ks * pc
            both = [re, im, HALF_ROOT * re[48:80], HALF_ROOT * im[48:80], jnp.zeros((32, 256), F32)]
            both = jnp.concatenate(both, axis=0)
            high = both.astype(BF)
            low = (both - high.astype(F32)).astype(BF)
            got = jnp.dot(inv, high, preferred_element_type=F32)
            got = (got + jnp.dot(inv, low, preferred_element_type=F32)).astype(BF)
            out_ref[:, r, x] = got[:, :128].reshape(16, 8, 128)
            out_ref[:, r, x + 1] = got[:, 128:].reshape(16, 8, 128)


def proj_kernel(pos_ref, e_ref, own, b1, lo, hi, b3, keep_ref, send_ref, buf, res):
    for x in range(4):
        for w in range(4):
            for y in range(4):
                row = 512 * x + 128 * w + 32 * y
                buf[row : row + 32] = e_ref[4 * y + w, :, x].reshape(32, 128).astype(F32)
    c = pos_ref[PC]
    for k in range(8):
        parts = [buf[pl.ds(pl.multiple_of(pos_ref[PX + j] * 512, 512) + k, 64, stride=8), :] for j in range(4)]
        left = jnp.concatenate(parts, axis=1).astype(BF)
        got = jnp.dot(left, points_of(k, own, b1, lo, hi, b3), preferred_element_type=F32)
        res[k] = got.reshape(4, 16, 256)
        for h in range(2):
            keep_ref[k, h] = res[k, 2 * h + c]
            send_ref[k, h] = res[k, 2 * h + 1 - c].astype(BF)


def body(orbitals, slab_points, kernel, twist_map):
    g, t = lax.axis_index("grp"), lax.axis_index("tw")
    x, h, c = g >> 2, (g >> 1) & 1, g & 1
    y = t >> 2
    pos = jnp.stack([128 * g, x, x ^ 1, x ^ 2, x ^ 3, y, y ^ 1, y ^ 2, y ^ 3, h, c]).astype(jnp.int32)

    b1 = lax.ppermute(orbitals, "grp", XMOVE[1])
    b3 = lax.ppermute(orbitals, "grp", XMOVE[3])

    *part, send, own = call(
        pick_kernel,
        [sds((8, 32, 256))] * 4 + [sds((8, 128, 256))] * 2,
        [SM, VM, VM],
        [pltpu.VMEM((256, 128), F32)],
        flops=10**8,
    )(pos, slab_points.reshape(2, 128), orbitals)
    recv = lax.ppermute(send, "grp", CORE)
    part = [p + recv[:, 32 * d : 32 * d + 32] for d, p in enumerate(part)]
    got = []
    for d in (1, 2, 3):
        got.append(lax.ppermute(part[d], "grp", XMOVE[d]))
    pieces = call(
        split_kernel, [sds((4, 128, 128))] * 4, [SM, VM], [pltpu.VMEM((2048, 128), F32)], flops=10**9
    )(pos, kernel)
    pieces = [pieces[0]] + [lax.ppermute(pieces[e], "tw", YMOVE[e]) for e in (1, 2, 3)]
    *got, p0, p1, p2, p3 = lax.optimization_barrier((*got, *pieces))
    total = part[0] + got[0] + got[1] + got[2]
    from_z = lax.ppermute(total, "grp", ZSWAP)
    lo = lax.ppermute(b3[:4], "grp", XMOVE[1])
    hi = lax.ppermute(b1[4:], "grp", XMOVE[3])
    fwd, inv = call(table_kernel, [sds((224, 128)), sds((128, 256))], [SM], flops=10**9)(twist_map)
    from_z, fwd, inv = lax.optimization_barrier((from_z, fwd, inv))
    pieces = call(
        turn_kernel, [sds((4, 128, 128))] * 4, [SM] + [VM] * 4, [pltpu.VMEM((4, 4, 128, 128), BF)]
    )(pos, p0, p1, p2, p3)
    pieces = [pieces[0]] + [lax.ppermute(pieces[d], "grp", XMOVE[d]) for d in (1, 2, 3)]
    total = total + from_z
    theirs = lax.ppermute(total, "grp", CORE)
    blocks = (own, b1, lo, hi, b3)
    pairs = call(
        pair_kernel, sds((16, 4, 4, 8, 128)), [SM] + [VM] * 7, [pltpu.VMEM((2048, 128), F32)], flops=10**8
    )(pos, total, theirs, *blocks)
    owned = lax.all_to_all(pairs, "tw", split_axis=0, concat_axis=0, tiled=True)
    owned, *pieces = lax.optimization_barrier((owned, *pieces))
    kc, ks = call(kernel_spectrum, [sds((4, 4, 80, 128), F32)] * 2, [SM] + [VM] * 5, flops=10**9)(pos, fwd, *pieces)
    exchange = call(conv_kernel, sds((16, 4, 4, 8, 128)), [VM] * 5, flops=10**9)(fwd, inv, kc, ks, owned)
    rows = lax.all_to_all(exchange, "tw", split_axis=0, concat_axis=0, tiled=True)
    keep, send = call(
        proj_kernel,
        [sds((8, 2, 16, 256), F32), sds((8, 2, 16, 256))],
        [SM] + [VM] * 6,
        [pltpu.VMEM((2048, 128), F32), pltpu.VMEM((8, 4, 16, 256), F32)],
        flops=10**8,
    )(pos, rows, *blocks)
    both = keep + lax.ppermute(send, "grp", CORE).astype(F32)
    z_send = lax.dynamic_index_in_dim(both, 1 - h, 1, keepdims=False).astype(BF)
    kept = lax.dynamic_index_in_dim(both, h, 1, keepdims=False)
    return (kept + lax.ppermute(z_send, "grp", ZSWAP).astype(F32)).astype(BF)


def solution(mesh):
    return jax.shard_map(
        body,
        mesh=mesh,
        in_specs=(P("tw", "grp", None), P(), P(None, "tw", "grp"), P()),
        out_specs=P("tw", "grp", None),
        check_vma=False,
    )
```

```python
import jax
import jax.numpy as jnp
from jax import lax
from jax.experimental import pallas as pl
from jax.experimental.pallas import tpu as pltpu
from jax.sharding import PartitionSpec as P


X, H, C, Y, W = 4, 2, 2, 4, 4
HALF_ROOT = 0.7071067811865476
BF, F32 = jnp.bfloat16, jnp.float32


VM = pl.BlockSpec(memory_space=pltpu.VMEM)
SM = pl.BlockSpec(memory_space=pltpu.SMEM)


def grp_perm(move):
    pairs = []
    for x in range(X):
        for h in range(H):
            for c in range(C):
                a, b, d = move(x, h, c)
                pairs.append(((x * H + h) * C + c, ((a % X) * H + b % H) * C + d % C))
    return pairs


CORE = grp_perm(lambda x, h, c: (x, h, c + 1))
ZSWAP = grp_perm(lambda x, h, c: (x, h + 1, c))
XMOVE = {d: grp_perm(lambda x, h, c, d=d: (x ^ d, h, c)) for d in (1, 2, 3)}
YMOVE = {e: [(t, t ^ (e * W)) for t in range(Y * W)] for e in (1, 2, 3)}

PX, PY, PH, PC = 0, 4, 8, 9


def call(kernel, outs, ins, scratch=(), flops=10**7, limit=24 << 20):
    return pl.pallas_call(
        kernel,
        out_shape=outs,
        in_specs=ins,
        out_specs=jax.tree.map(lambda _: VM, outs),
        scratch_shapes=list(scratch),
        compiler_params=pltpu.CompilerParams(vmem_limit_bytes=limit),
        cost_estimate=pl.CostEstimate(flops=flops, bytes_accessed=10**6, transcendentals=0),
    )


def sds(shape, dtype=BF):
    return jax.ShapeDtypeStruct(shape, dtype)


def far_kernel(pos_ref, pts_ref, own_ref, keep_ref, send_ref, hot_ref, copy_ref, buf):
    c = pos_ref[PC]
    sub = lax.broadcasted_iota(jnp.int32, (128, 64), 0)

    def hot(chunk, block):
        pts = pts_ref[pl.ds(pos_ref[PX + chunk], 1)]
        base = 512 * pos_ref[PX + block] + 256 * pos_ref[PH] + 128 * c
        buf[...] = (pts == sub + base).astype(F32).T
        halves = [buf[pl.ds(pl.multiple_of(32 * i, 32), 32)] for i in (c, 1 - c)]
        return jnp.concatenate(halves, axis=0).astype(BF)

    rows = hot(2, 0)
    for k in range(8):
        got = jnp.dot(rows, own_ref[k], preferred_element_type=F32).astype(BF)
        keep_ref[k] = got[:32]
        send_ref[k] = got[32:]
    copy_ref[...] = own_ref[...]
    for i, block in enumerate((0, 1, 3)):
        hot_ref[:, 128 * i : 128 * i + 128] = hot(0, block)


def near_kernel(hot_ref, own, b1, b3, far_ref, keep_ref, send_ref):
    rows = hot_ref[...]
    for k in range(8):
        points = jnp.concatenate([own[k], b1[k], b3[k]], axis=0)
        got = jnp.dot(rows, points, preferred_element_type=F32)
        keep_ref[k] = (got[:32] + far_ref[k].astype(F32)).astype(BF)
        send_ref[k] = got[32:].astype(BF)


def points_of(k, own, b1, lo, hi, b3):
    two = lo[k] if k < 4 else hi[k - 4]
    return jnp.concatenate([own[k], b1[k], two, b3[k]], axis=0)


def pair_kernel(pos_ref, mine, theirs, own, b1, lo, hi, b3, out_ref, buf):
    c = pos_ref[PC]
    for k in range(8):
        left = jnp.concatenate([mine[k], theirs[k]], axis=0)
        right = points_of(k, own, b1, lo, hi, b3)
        got = lax.dot_general(left, right, (((1,), (1,)), ((), ())), preferred_element_type=F32)
        for j in range(4):
            for i, half in enumerate((c, 1 - c)):
                base = pl.multiple_of(pos_ref[PX + j] * 512 + half * 256, 256)
                buf[pl.ds(base + k, 32, stride=8), :] = got[32 * i : 32 * i + 32, 128 * j : 128 * j + 128]
    for x in range(4):
        for w in range(4):
            for y in range(4):
                row = 512 * x + 128 * w + 32 * y
                out_ref[4 * y + w, :, x] = buf[row : row + 32].reshape(4, 8, 128).astype(BF)


def table_kernel(map_ref, fwd_ref, inv_ref):
    e = map_ref[0, 0]

    def neg(a):
        return map_ref[e, a]

    def add(a, b):
        return map_ref[a, neg(b)]

    def dbl(a):
        return map_ref[a, neg(a)]

    def find(ok):
        return lax.while_loop(lambda l: jnp.logical_and(l < 127, jnp.logical_not(ok(l))), lambda l: l + 1, jnp.int32(0))

    def c_ok(l):
        return dbl(dbl(l)) != e

    c = find(c_ok)
    c4 = dbl(dbl(c))

    def a_ok(l):
        d = dbl(l)
        return (dbl(d) == e) & (d != e) & (d != c4)

    a = find(a_ok)
    a2 = dbl(a)
    ac = add(a2, c4)

    def b_ok(l):
        d = dbl(l)
        return (dbl(d) == e) & (d != e) & (d != c4) & (d != a2) & (d != ac)

    b = find(b_ok)
    na, nb, nc = neg(a), neg(b), neg(c)
    lane = lax.broadcasted_iota(jnp.int32, (8, 128), 1)

    def walk(n, carry):
        cur, where = carry
        where = jnp.where(lane == cur, n, where)
        cur = map_ref[cur, nc]
        cur = jnp.where(n % 8 == 7, map_ref[cur, nb], cur)
        cur = jnp.where(n % 32 == 31, map_ref[cur, na], cur)
        return cur, where

    _, where = lax.fori_loop(0, 128, walk, (e, jnp.zeros((8, 128), jnp.int32)))
    where = where[0:1]
    li, lj, ll = where // 32, (where // 8) % 4, where % 8
    row = lax.broadcasted_iota(jnp.int32, (80, 128), 0)
    fi, fj = (row // 4) % 4, row % 4
    fl = jnp.where(row < 48, 2 * (row // 16), 2 * (row // 16) - 5)
    turn = (2 * fi * li + 2 * fj * lj + fl * ll) % 8

    def parts(m):
        whole = jnp.where(m == 0, 1.0, 0.0) - jnp.where(m == 4, 1.0, 0.0)
        root = jnp.where((m == 1) | (m == 7), 1.0, 0.0) - jnp.where((m == 3) | (m == 5), 1.0, 0.0)
        return whole, root[48:80]

    cw, cr = parts(turn)
    sw, sr = parts((turn + 6) % 8)
    whole = jnp.concatenate([cw, sw, cr, sr, jnp.zeros((32, 128), F32)], axis=0)
    fwd_ref[...] = whole[0:224].astype(BF)
    inv_ref[...] = whole.T.astype(BF)


def with_root(got, root):
    return jnp.concatenate([got[0:48], got[48:80] + HALF_ROOT * root], axis=0)


def spectrum(fwd, cols):
    got = jnp.dot(fwd, cols, preferred_element_type=F32)
    return with_root(got[0:80], got[160:192]), with_root(got[80:160], got[192:224])


def split_kernel(pos_ref, k_ref, o0, o1, o2, o3, buf):
    buf[...] = k_ref[...].reshape(2048, 128).astype(F32)
    for e, ref in enumerate((o0, o1, o2, o3)):
        for r in range(4):
            ref[r] = buf[pl.ds(4 * pos_ref[PY + e] + r, 128, stride=16), :].astype(BF)


def turn_kernel(pos_ref, p0, p1, p2, p3, o0, o1, o2, o3, buf):
    for e, ref in enumerate((p0, p1, p2, p3)):
        buf[e] = ref[...]
    y = pos_ref[PY]
    for d, ref in enumerate((o0, o1, o2, o3)):
        ref[...] = buf[y ^ pos_ref[PX + d]]


def kernel_spectrum(pos_ref, fwd_ref, p0, p1, p2, p3, cos_ref, sin_ref):
    fwd = fwd_ref[...]
    row = lax.broadcasted_iota(jnp.int32, (80, 256), 0)
    alone = (row < 16) | ((row >= 32) & (row < 48))
    scale = jnp.where(alone, 1.0 / 128**2, 2.0 / 128**2)
    for e, (one, two) in ((0, (p0, p1)), (2, (p2, p3))):
        for r in range(4):
            cos, sin = spectrum(fwd, jnp.concatenate([one[r], two[r]], axis=1))
            cos, sin = cos * scale, sin * scale
            for i in range(2):
                x = pos_ref[PX + e + i]
                cos_ref[x, r] = cos[:, 128 * i : 128 * i + 128]
                sin_ref[x, r] = sin[:, 128 * i : 128 * i + 128]


def conv_kernel(fwd_ref, inv_ref, kc_ref, ks_ref, p_ref, out_ref):
    fwd, inv = fwd_ref[...], inv_ref[...]
    for r in range(4):
        for x in (0, 2):
            cols = jnp.concatenate([p_ref[:, r, x].reshape(128, 128), p_ref[:, r, x + 1].reshape(128, 128)], axis=1)
            pc, ps = spectrum(fwd, cols)
            kc = jnp.concatenate([kc_ref[x, r], kc_ref[x + 1, r]], axis=1)
            ks = jnp.concatenate([ks_ref[x, r], ks_ref[x + 1, r]], axis=1)
            re = kc * pc - ks * ps
            im = kc * ps + ks * pc
            both = [re, im, HALF_ROOT * re[48:80], HALF_ROOT * im[48:80], jnp.zeros((32, 256), F32)]
            both = jnp.concatenate(both, axis=0)
            high = both.astype(BF)
            low = (both - high.astype(F32)).astype(BF)
            got = jnp.dot(inv, high, preferred_element_type=F32)
            got = (got + jnp.dot(inv, low, preferred_element_type=F32)).astype(BF)
            out_ref[:, r, x] = got[:, :128].reshape(16, 8, 128)
            out_ref[:, r, x + 1] = got[:, 128:].reshape(16, 8, 128)


def proj_kernel(pos_ref, e_ref, own, b1, lo, hi, b3, keep_ref, send_ref, buf, res):
    for x in range(4):
        for w in range(4):
            for y in range(4):
                row = 512 * x + 128 * w + 32 * y
                buf[row : row + 32] = e_ref[4 * y + w, :, x].reshape(32, 128).astype(F32)
    c = pos_ref[PC]
    for k in range(8):
        parts = [buf[pl.ds(pl.multiple_of(pos_ref[PX + j] * 512, 512) + k, 64, stride=8), :] for j in range(4)]
        left = jnp.concatenate(parts, axis=1).astype(BF)
        got = jnp.dot(left, points_of(k, own, b1, lo, hi, b3), preferred_element_type=F32)
        res[k] = got.reshape(4, 16, 256)
        for h in range(2):
            keep_ref[k, h] = res[k, 2 * h + c]
            send_ref[k, h] = res[k, 2 * h + 1 - c].astype(BF)


def body(orbitals, slab_points, kernel, twist_map):
    g, t = lax.axis_index("grp"), lax.axis_index("tw")
    x, h, c = g >> 2, (g >> 1) & 1, g & 1
    y = t >> 2
    pos = jnp.stack([x, x ^ 1, x ^ 2, x ^ 3, y, y ^ 1, y ^ 2, y ^ 3, h, c]).astype(jnp.int32)

    b1 = lax.ppermute(orbitals, "grp", XMOVE[1])
    b3 = lax.ppermute(orbitals, "grp", XMOVE[3])

    part = sds((8, 32, 256))
    far, send, hot, own = call(
        far_kernel,
        [part, part, sds((64, 384)), sds((8, 128, 256))],
        [SM, VM, VM],
        [pltpu.VMEM((64, 128), F32)],
        flops=10**8,
    )(pos, slab_points.reshape(4, 64), orbitals)
    far = far + lax.ppermute(send, "grp", CORE)
    far = lax.ppermute(far, "grp", XMOVE[2])
    pieces = call(
        split_kernel, [sds((4, 128, 128))] * 4, [SM, VM], [pltpu.VMEM((2048, 128), F32)], flops=10**9
    )(pos, kernel)
    pieces = [pieces[0]] + [lax.ppermute(pieces[e], "tw", YMOVE[e]) for e in (1, 2, 3)]
    pieces = call(
        turn_kernel, [sds((4, 128, 128))] * 4, [SM] + [VM] * 4, [pltpu.VMEM((4, 4, 128, 128), BF)]
    )(pos, *pieces)
    far, *pieces = lax.optimization_barrier((far, *pieces))
    total, send = call(near_kernel, [part, part], [VM] * 5, flops=10**8)(hot, own, b1, b3, far)
    recv = lax.ppermute(send, "grp", CORE)
    lo = lax.ppermute(b3[:4], "grp", XMOVE[1])
    hi = lax.ppermute(b1[4:], "grp", XMOVE[3])
    total = total + recv
    from_z = lax.ppermute(total, "grp", ZSWAP)
    fwd, inv = call(table_kernel, [sds((224, 128)), sds((128, 256))], [SM], flops=10**9)(twist_map)
    moved = [pieces[0]]
    for d in (1, 2, 3):
        moved.append(lax.ppermute(pieces[d], "grp", XMOVE[d]))
    pieces = moved
    total = total + from_z
    theirs = lax.ppermute(total, "grp", CORE)
    blocks = (own, b1, lo, hi, b3)
    pairs = call(
        pair_kernel, sds((16, 4, 4, 8, 128)), [SM] + [VM] * 7, [pltpu.VMEM((2048, 128), F32)], flops=10**8
    )(pos, total, theirs, *blocks)
    owned = lax.all_to_all(pairs, "tw", split_axis=0, concat_axis=0, tiled=True)
    owned, *pieces = lax.optimization_barrier((owned, *pieces))
    kc, ks = call(kernel_spectrum, [sds((4, 4, 80, 128), F32)] * 2, [SM] + [VM] * 5, flops=10**9)(pos, fwd, *pieces)
    exchange = call(conv_kernel, sds((16, 4, 4, 8, 128)), [VM] * 5, flops=10**9)(fwd, inv, kc, ks, owned)
    rows = lax.all_to_all(exchange, "tw", split_axis=0, concat_axis=0, tiled=True)
    keep, send = call(
        proj_kernel,
        [sds((8, 2, 16, 256), F32), sds((8, 2, 16, 256))],
        [SM] + [VM] * 6,
        [pltpu.VMEM((2048, 128), F32), pltpu.VMEM((8, 4, 16, 256), F32)],
        flops=10**8,
    )(pos, rows, orbitals, *blocks[1:])
    both = keep + lax.ppermute(send, "grp", CORE).astype(F32)
    z_send = lax.dynamic_index_in_dim(both, 1 - h, 1, keepdims=False).astype(BF)
    kept = lax.dynamic_index_in_dim(both, h, 1, keepdims=False)
    return (kept + lax.ppermute(z_send, "grp", ZSWAP).astype(F32)).astype(BF)


def solution(mesh):
    return jax.shard_map(
        body,
        mesh=mesh,
        in_specs=(P("tw", "grp", None), P(), P(None, "tw", "grp"), P()),
        out_specs=P("tw", "grp", None),
        check_vma=False,
    )
```

```python
import jax
import jax.numpy as jnp
from jax import lax
from jax.experimental import pallas as pl
from jax.experimental.pallas import tpu as pltpu
from jax.sharding import PartitionSpec as P


X, H, C, Y, W = 4, 2, 2, 4, 4
HALF_ROOT = 0.7071067811865476
BF, F32 = jnp.bfloat16, jnp.float32


VM = pl.BlockSpec(memory_space=pltpu.VMEM)
SM = pl.BlockSpec(memory_space=pltpu.SMEM)


def grp_perm(move):
    pairs = []
    for x in range(X):
        for h in range(H):
            for c in range(C):
                a, b, d = move(x, h, c)
                pairs.append(((x * H + h) * C + c, ((a % X) * H + b % H) * C + d % C))
    return pairs


CORE = grp_perm(lambda x, h, c: (x, h, c + 1))
ZSWAP = grp_perm(lambda x, h, c: (x, h + 1, c))
XMOVE = {d: grp_perm(lambda x, h, c, d=d: (x ^ d, h, c)) for d in (1, 2, 3)}
YMOVE = {e: [(t, t ^ (e * W)) for t in range(Y * W)] for e in (1, 2, 3)}

PX, PY, PH, PC = 0, 4, 8, 9


def call(kernel, outs, ins, scratch=(), flops=10**7, limit=24 << 20):
    return pl.pallas_call(
        kernel,
        out_shape=outs,
        in_specs=ins,
        out_specs=jax.tree.map(lambda _: VM, outs),
        scratch_shapes=list(scratch),
        compiler_params=pltpu.CompilerParams(vmem_limit_bytes=limit),
        cost_estimate=pl.CostEstimate(flops=flops, bytes_accessed=10**6, transcendentals=0),
    )


def sds(shape, dtype=BF):
    return jax.ShapeDtypeStruct(shape, dtype)


def far_kernel(pos_ref, pts_ref, own_ref, keep_ref, send_ref, hot_ref, copy_ref, buf):
    c = pos_ref[PC]
    sub = lax.broadcasted_iota(jnp.int32, (128, 64), 0)

    def hot(chunk, block):
        pts = pts_ref[pl.ds(pos_ref[PX + chunk], 1)]
        base = 512 * pos_ref[PX + block] + 256 * pos_ref[PH] + 128 * c
        buf[...] = (pts == sub + base).astype(F32).T
        halves = [buf[pl.ds(pl.multiple_of(32 * i, 32), 32)] for i in (c, 1 - c)]
        return jnp.concatenate(halves, axis=0).astype(BF)

    rows = hot(2, 0)
    for k in range(8):
        got = jnp.dot(rows, own_ref[k], preferred_element_type=F32).astype(BF)
        keep_ref[k] = got[:32]
        send_ref[k] = got[32:]
    copy_ref[...] = own_ref[...]
    for i, block in enumerate((0, 1, 3)):
        hot_ref[:, 128 * i : 128 * i + 128] = hot(0, block)


def near_kernel(hot_ref, own, b1, b3, far_ref, keep_ref, send_ref):
    rows = hot_ref[...]
    for k in range(8):
        points = jnp.concatenate([own[k], b1[k], b3[k]], axis=0)
        got = jnp.dot(rows, points, preferred_element_type=F32)
        keep_ref[k] = (got[:32] + far_ref[k].astype(F32)).astype(BF)
        send_ref[k] = got[32:].astype(BF)


def points_of(k, own, b1, lo, hi, b3):
    two = lo[k] if k < 4 else hi[k - 4]
    return jnp.concatenate([own[k], b1[k], two, b3[k]], axis=0)


def pair_kernel(pos_ref, mine, theirs, own, b1, lo, hi, b3, out_ref, buf):
    c = pos_ref[PC]
    for k in range(8):
        left = jnp.concatenate([mine[k], theirs[k]], axis=0)
        right = points_of(k, own, b1, lo, hi, b3)
        got = lax.dot_general(left, right, (((1,), (1,)), ((), ())), preferred_element_type=F32)
        for j in range(4):
            for i, half in enumerate((c, 1 - c)):
                base = pl.multiple_of(pos_ref[PX + j] * 512 + half * 256, 256)
                buf[pl.ds(base + k, 32, stride=8), :] = got[32 * i : 32 * i + 32, 128 * j : 128 * j + 128]
    for x in range(4):
        for w in range(4):
            for y in range(4):
                row = 512 * x + 128 * w + 32 * y
                out_ref[4 * y + w, :, x] = buf[row : row + 32].reshape(4, 8, 128).astype(BF)


def table_kernel(map_ref, fwd_ref, inv_ref):
    e = map_ref[0, 0]

    def neg(a):
        return map_ref[e, a]

    def add(a, b):
        return map_ref[a, neg(b)]

    def dbl(a):
        return map_ref[a, neg(a)]

    def find(ok):
        return lax.while_loop(lambda l: jnp.logical_and(l < 127, jnp.logical_not(ok(l))), lambda l: l + 1, jnp.int32(0))

    def c_ok(l):
        return dbl(dbl(l)) != e

    c = find(c_ok)
    c4 = dbl(dbl(c))

    def a_ok(l):
        d = dbl(l)
        return (dbl(d) == e) & (d != e) & (d != c4)

    a = find(a_ok)
    a2 = dbl(a)
    ac = add(a2, c4)

    def b_ok(l):
        d = dbl(l)
        return (dbl(d) == e) & (d != e) & (d != c4) & (d != a2) & (d != ac)

    b = find(b_ok)
    na, nb, nc = neg(a), neg(b), neg(c)
    lane = lax.broadcasted_iota(jnp.int32, (8, 128), 1)

    def walk(n, carry):
        cur, where = carry
        where = jnp.where(lane == cur, n, where)
        cur = map_ref[cur, nc]
        cur = jnp.where(n % 8 == 7, map_ref[cur, nb], cur)
        cur = jnp.where(n % 32 == 31, map_ref[cur, na], cur)
        return cur, where

    _, where = lax.fori_loop(0, 128, walk, (e, jnp.zeros((8, 128), jnp.int32)))
    where = where[0:1]
    li, lj, ll = where // 32, (where // 8) % 4, where % 8
    row = lax.broadcasted_iota(jnp.int32, (80, 128), 0)
    fi, fj = (row // 4) % 4, row % 4
    fl = jnp.where(row < 48, 2 * (row // 16), 2 * (row // 16) - 5)
    turn = (2 * fi * li + 2 * fj * lj + fl * ll) % 8

    def parts(m):
        whole = jnp.where(m == 0, 1.0, 0.0) - jnp.where(m == 4, 1.0, 0.0)
        root = jnp.where((m == 1) | (m == 7), 1.0, 0.0) - jnp.where((m == 3) | (m == 5), 1.0, 0.0)
        return whole, root[48:80]

    cw, cr = parts(turn)
    sw, sr = parts((turn + 6) % 8)
    whole = jnp.concatenate([cw, sw, cr, sr, jnp.zeros((32, 128), F32)], axis=0)
    fwd_ref[...] = whole[0:224].astype(BF)
    inv_ref[...] = whole.T.astype(BF)


def with_root(got, root):
    return jnp.concatenate([got[0:48], got[48:80] + HALF_ROOT * root], axis=0)


def spectrum(fwd, cols):
    got = jnp.dot(fwd, cols, preferred_element_type=F32)
    return with_root(got[0:80], got[160:192]), with_root(got[80:160], got[192:224])


def split_kernel(pos_ref, k_ref, o0, o1, o2, o3, buf):
    buf[...] = k_ref[...].reshape(2048, 128).astype(F32)
    for e, ref in enumerate((o0, o1, o2, o3)):
        for r in range(4):
            ref[r] = buf[pl.ds(4 * pos_ref[PY + e] + r, 128, stride=16), :].astype(BF)


def turn_kernel(pos_ref, p0, p1, p2, p3, o0, o1, o2, o3, buf):
    for e, ref in enumerate((p0, p1, p2, p3)):
        buf[e] = ref[...]
    y = pos_ref[PY]
    for d, ref in enumerate((o0, o1, o2, o3)):
        ref[...] = buf[y ^ pos_ref[PX + d]]


def kernel_spectrum(pos_ref, fwd_ref, p0, p1, p2, p3, cos_ref, sin_ref):
    fwd = fwd_ref[...]
    row = lax.broadcasted_iota(jnp.int32, (80, 256), 0)
    alone = (row < 16) | ((row >= 32) & (row < 48))
    scale = jnp.where(alone, 1.0 / 128**2, 2.0 / 128**2)
    for e, (one, two) in ((0, (p0, p1)), (2, (p2, p3))):
        for r in range(4):
            cos, sin = spectrum(fwd, jnp.concatenate([one[r], two[r]], axis=1))
            cos, sin = cos * scale, sin * scale
            for i in range(2):
                x = pos_ref[PX + e + i]
                cos_ref[x, r] = cos[:, 128 * i : 128 * i + 128]
                sin_ref[x, r] = sin[:, 128 * i : 128 * i + 128]


def conv_kernel(fwd_ref, inv_ref, kc_ref, ks_ref, p_ref, out_ref):
    fwd, inv = fwd_ref[...], inv_ref[...]
    for r in range(4):
        for x in (0, 2):
            cols = jnp.concatenate([p_ref[:, r, x].reshape(128, 128), p_ref[:, r, x + 1].reshape(128, 128)], axis=1)
            pc, ps = spectrum(fwd, cols)
            kc = jnp.concatenate([kc_ref[x, r], kc_ref[x + 1, r]], axis=1)
            ks = jnp.concatenate([ks_ref[x, r], ks_ref[x + 1, r]], axis=1)
            re = kc * pc - ks * ps
            im = kc * ps + ks * pc
            both = [re, im, HALF_ROOT * re[48:80], HALF_ROOT * im[48:80], jnp.zeros((32, 256), F32)]
            both = jnp.concatenate(both, axis=0)
            high = both.astype(BF)
            low = (both - high.astype(F32)).astype(BF)
            got = jnp.dot(inv, high, preferred_element_type=F32)
            got = (got + jnp.dot(inv, low, preferred_element_type=F32)).astype(BF)
            out_ref[:, r, x] = got[:, :128].reshape(16, 8, 128)
            out_ref[:, r, x + 1] = got[:, 128:].reshape(16, 8, 128)


def proj_kernel(pos_ref, e_ref, own, b1, lo, hi, b3, keep_ref, send_ref, buf, res):
    for x in range(4):
        for w in range(4):
            for y in range(4):
                row = 512 * x + 128 * w + 32 * y
                buf[row : row + 32] = e_ref[4 * y + w, :, x].reshape(32, 128).astype(F32)
    c = pos_ref[PC]
    for k in range(8):
        parts = [buf[pl.ds(pl.multiple_of(pos_ref[PX + j] * 512, 512) + k, 64, stride=8), :] for j in range(4)]
        left = jnp.concatenate(parts, axis=1).astype(BF)
        got = jnp.dot(left, points_of(k, own, b1, lo, hi, b3), preferred_element_type=F32)
        res[k] = got.reshape(4, 16, 256)
        for h in range(2):
            keep_ref[k, h] = res[k, 2 * h + c]
            send_ref[k, h] = res[k, 2 * h + 1 - c].astype(BF)


def body(orbitals, slab_points, kernel, twist_map):
    g, t = lax.axis_index("grp"), lax.axis_index("tw")
    x, h, c = g >> 2, (g >> 1) & 1, g & 1
    y = t >> 2
    pos = jnp.stack([x, x ^ 1, x ^ 2, x ^ 3, y, y ^ 1, y ^ 2, y ^ 3, h, c]).astype(jnp.int32)

    b1 = lax.ppermute(orbitals, "grp", XMOVE[1])
    b3 = lax.ppermute(orbitals, "grp", XMOVE[3])

    part = sds((8, 32, 256))
    far, send, hot, own = call(
        far_kernel,
        [part, part, sds((64, 384)), sds((8, 128, 256))],
        [SM, VM, VM],
        [pltpu.VMEM((64, 128), F32)],
        flops=10**8,
    )(pos, slab_points.reshape(4, 64), orbitals)
    far = far + lax.ppermute(send, "grp", CORE)
    far = lax.ppermute(far, "grp", XMOVE[2])
    pieces = call(
        split_kernel, [sds((4, 128, 128))] * 4, [SM, VM], [pltpu.VMEM((2048, 128), F32)], flops=10**9
    )(pos, kernel)
    moved = [pieces[0]]
    for e in (1, 2, 3):
        moved.append(lax.ppermute(pieces[e], "tw", YMOVE[e]))
    pieces = moved
    total, send = call(near_kernel, [part, part], [VM] * 5, flops=10**8)(hot, own, b1, b3, far)
    recv = lax.ppermute(send, "grp", CORE)
    lo = lax.ppermute(b3[:4], "grp", XMOVE[1])
    hi = lax.ppermute(b1[4:], "grp", XMOVE[3])
    total = total + recv
    from_z = lax.ppermute(total, "grp", ZSWAP)
    fwd, inv = call(table_kernel, [sds((224, 128)), sds((128, 256))], [SM], flops=10**9)(twist_map)
    pieces = call(
        turn_kernel, [sds((4, 128, 128))] * 4, [SM] + [VM] * 4, [pltpu.VMEM((4, 4, 128, 128), BF)]
    )(pos, *pieces)
    moved = [pieces[0]]
    for d in (1, 2, 3):
        moved.append(lax.ppermute(pieces[d], "grp", XMOVE[d]))
    pieces = moved
    total = total + from_z
    theirs = lax.ppermute(total, "grp", CORE)
    blocks = (own, b1, lo, hi, b3)
    pairs = call(
        pair_kernel, sds((16, 4, 4, 8, 128)), [SM] + [VM] * 7, [pltpu.VMEM((2048, 128), F32)], flops=10**8
    )(pos, total, theirs, *blocks)
    owned = lax.all_to_all(pairs, "tw", split_axis=0, concat_axis=0, tiled=True)
    owned, *pieces = lax.optimization_barrier((owned, *pieces))
    kc, ks = call(kernel_spectrum, [sds((4, 4, 80, 128), F32)] * 2, [SM] + [VM] * 5, flops=10**9)(pos, fwd, *pieces)
    exchange = call(conv_kernel, sds((16, 4, 4, 8, 128)), [VM] * 5, flops=10**9)(fwd, inv, kc, ks, owned)
    rows = lax.all_to_all(exchange, "tw", split_axis=0, concat_axis=0, tiled=True)
    keep, send = call(
        proj_kernel,
        [sds((8, 2, 16, 256), F32), sds((8, 2, 16, 256))],
        [SM] + [VM] * 6,
        [pltpu.VMEM((2048, 128), F32), pltpu.VMEM((8, 4, 16, 256), F32)],
        flops=10**8,
    )(pos, rows, orbitals, *blocks[1:])
    both = keep + lax.ppermute(send, "grp", CORE).astype(F32)
    z_send = lax.dynamic_index_in_dim(both, 1 - h, 1, keepdims=False).astype(BF)
    kept = lax.dynamic_index_in_dim(both, h, 1, keepdims=False)
    return (kept + lax.ppermute(z_send, "grp", ZSWAP).astype(F32)).astype(BF)


def solution(mesh):
    return jax.shard_map(
        body,
        mesh=mesh,
        in_specs=(P("tw", "grp", None), P(), P(None, "tw", "grp"), P()),
        out_specs=P("tw", "grp", None),
        check_vma=False,
    )
```

```python
import jax
import jax.numpy as jnp
from jax import lax
from jax.experimental import pallas as pl
from jax.experimental.pallas import tpu as pltpu
from jax.sharding import PartitionSpec as P


X, H, C, Y, W = 4, 2, 2, 4, 4
HALF_ROOT = 0.7071067811865476
BF, F32 = jnp.bfloat16, jnp.float32


VM = pl.BlockSpec(memory_space=pltpu.VMEM)
SM = pl.BlockSpec(memory_space=pltpu.SMEM)
ANY = pl.BlockSpec(memory_space=pltpu.HBM)


def grp_perm(move):
    pairs = []
    for x in range(X):
        for h in range(H):
            for c in range(C):
                a, b, d = move(x, h, c)
                pairs.append(((x * H + h) * C + c, ((a % X) * H + b % H) * C + d % C))
    return pairs


CORE = grp_perm(lambda x, h, c: (x, h, c + 1))
ZSWAP = grp_perm(lambda x, h, c: (x, h + 1, c))
XMOVE = {d: grp_perm(lambda x, h, c, d=d: (x ^ d, h, c)) for d in (1, 2, 3)}
YMOVE = {e: [(t, t ^ (e * W)) for t in range(Y * W)] for e in (1, 2, 3)}

PX, PY, PH, PC = 0, 4, 8, 9


def call(kernel, outs, ins, scratch=(), flops=10**7, limit=24 << 20):
    return pl.pallas_call(
        kernel,
        out_shape=outs,
        in_specs=ins,
        out_specs=jax.tree.map(lambda _: VM, outs),
        scratch_shapes=list(scratch),
        compiler_params=pltpu.CompilerParams(vmem_limit_bytes=limit),
        cost_estimate=pl.CostEstimate(flops=flops, bytes_accessed=10**6, transcendentals=0),
    )


def sds(shape, dtype=BF):
    return jax.ShapeDtypeStruct(shape, dtype)


def far_kernel(pos_ref, pts_hbm, own_hbm, keep_ref, send_ref, hot_ref, own_ref, buf, pts_ref, sem):
    load_points = pltpu.make_async_copy(pts_hbm, pts_ref, sem.at[0])
    load_own = pltpu.make_async_copy(own_hbm, own_ref, sem.at[1])
    load_points.start()
    load_own.start()
    c = pos_ref[PC]
    sub = lax.broadcasted_iota(jnp.int32, (128, 64), 0)
    load_points.wait()

    def hot(chunk, block):
        pts = pts_ref[pl.ds(pos_ref[PX + chunk], 1)]
        base = 512 * pos_ref[PX + block] + 256 * pos_ref[PH] + 128 * c
        buf[...] = (pts == sub + base).astype(F32).T
        halves = [buf[pl.ds(pl.multiple_of(32 * i, 32), 32)] for i in (c, 1 - c)]
        return jnp.concatenate(halves, axis=0).astype(BF)

    rows = hot(2, 0)
    load_own.wait()
    for k in range(8):
        got = jnp.dot(rows, own_ref[k], preferred_element_type=F32).astype(BF)
        keep_ref[k] = got[:32]
        send_ref[k] = got[32:]
    for i, block in enumerate((0, 1, 3)):
        hot_ref[:, 128 * i : 128 * i + 128] = hot(0, block)


def near_kernel(hot_ref, own, b1, b3, far_ref, keep_ref, send_ref):
    rows = hot_ref[...]
    for k in range(8):
        points = jnp.concatenate([own[k], b1[k], b3[k]], axis=0)
        got = jnp.dot(rows, points, preferred_element_type=F32)
        keep_ref[k] = (got[:32] + far_ref[k].astype(F32)).astype(BF)
        send_ref[k] = got[32:].astype(BF)


def points_of(k, own, b1, lo, hi, b3):
    two = lo[k] if k < 4 else hi[k - 4]
    return jnp.concatenate([own[k], b1[k], two, b3[k]], axis=0)


def pair_kernel(pos_ref, mine, theirs, own, b1, lo, hi, b3, out_ref, buf):
    c = pos_ref[PC]
    for k in range(8):
        left = jnp.concatenate([mine[k], theirs[k]], axis=0)
        right = points_of(k, own, b1, lo, hi, b3)
        got = lax.dot_general(left, right, (((1,), (1,)), ((), ())), preferred_element_type=F32)
        for j in range(4):
            for i, half in enumerate((c, 1 - c)):
                base = pl.multiple_of(pos_ref[PX + j] * 512 + half * 256, 256)
                buf[pl.ds(base + k, 32, stride=8), :] = got[32 * i : 32 * i + 32, 128 * j : 128 * j + 128]
    for x in range(4):
        for w in range(4):
            for y in range(4):
                row = 512 * x + 128 * w + 32 * y
                out_ref[4 * y + w, :, x] = buf[row : row + 32].reshape(4, 8, 128).astype(BF)


def table_kernel(map_ref, fwd_ref, inv_ref):
    e = map_ref[0, 0]

    def neg(a):
        return map_ref[e, a]

    def add(a, b):
        return map_ref[a, neg(b)]

    def dbl(a):
        return map_ref[a, neg(a)]

    def find(ok):
        return lax.while_loop(lambda l: jnp.logical_and(l < 127, jnp.logical_not(ok(l))), lambda l: l + 1, jnp.int32(0))

    def c_ok(l):
        return dbl(dbl(l)) != e

    c = find(c_ok)
    c4 = dbl(dbl(c))

    def a_ok(l):
        d = dbl(l)
        return (dbl(d) == e) & (d != e) & (d != c4)

    a = find(a_ok)
    a2 = dbl(a)
    ac = add(a2, c4)

    def b_ok(l):
        d = dbl(l)
        return (dbl(d) == e) & (d != e) & (d != c4) & (d != a2) & (d != ac)

    b = find(b_ok)
    na, nb, nc = neg(a), neg(b), neg(c)
    lane = lax.broadcasted_iota(jnp.int32, (8, 128), 1)

    def walk(n, carry):
        cur, where = carry
        where = jnp.where(lane == cur, n, where)
        cur = map_ref[cur, nc]
        cur = jnp.where(n % 8 == 7, map_ref[cur, nb], cur)
        cur = jnp.where(n % 32 == 31, map_ref[cur, na], cur)
        return cur, where

    _, where = lax.fori_loop(0, 128, walk, (e, jnp.zeros((8, 128), jnp.int32)))
    where = where[0:1]
    li, lj, ll = where // 32, (where // 8) % 4, where % 8
    row = lax.broadcasted_iota(jnp.int32, (80, 128), 0)
    fi, fj = (row // 4) % 4, row % 4
    fl = jnp.where(row < 48, 2 * (row // 16), 2 * (row // 16) - 5)
    turn = (2 * fi * li + 2 * fj * lj + fl * ll) % 8

    def parts(m):
        whole = jnp.where(m == 0, 1.0, 0.0) - jnp.where(m == 4, 1.0, 0.0)
        root = jnp.where((m == 1) | (m == 7), 1.0, 0.0) - jnp.where((m == 3) | (m == 5), 1.0, 0.0)
        return whole, root[48:80]

    cw, cr = parts(turn)
    sw, sr = parts((turn + 6) % 8)
    whole = jnp.concatenate([cw, sw, cr, sr, jnp.zeros((32, 128), F32)], axis=0)
    fwd_ref[...] = whole[0:224].astype(BF)
    inv_ref[...] = whole.T.astype(BF)


def with_root(got, root):
    return jnp.concatenate([got[0:48], got[48:80] + HALF_ROOT * root], axis=0)


def spectrum(fwd, cols):
    got = jnp.dot(fwd, cols, preferred_element_type=F32)
    return with_root(got[0:80], got[160:192]), with_root(got[80:160], got[192:224])


def split_kernel(pos_ref, k_ref, o0, o1, o2, o3, buf):
    buf[...] = k_ref[...].reshape(2048, 128).astype(F32)
    for e, ref in enumerate((o0, o1, o2, o3)):
        for r in range(4):
            ref[r] = buf[pl.ds(4 * pos_ref[PY + e] + r, 128, stride=16), :].astype(BF)


def turn_kernel(pos_ref, p0, p1, p2, p3, o0, o1, o2, o3, buf):
    for e, ref in enumerate((p0, p1, p2, p3)):
        buf[e] = ref[...]
    y = pos_ref[PY]
    for d, ref in enumerate((o0, o1, o2, o3)):
        ref[...] = buf[y ^ pos_ref[PX + d]]


def kernel_spectrum(pos_ref, fwd_ref, p0, p1, p2, p3, cos_ref, sin_ref):
    fwd = fwd_ref[...]
    row = lax.broadcasted_iota(jnp.int32, (80, 256), 0)
    alone = (row < 16) | ((row >= 32) & (row < 48))
    scale = jnp.where(alone, 1.0 / 128**2, 2.0 / 128**2)
    for e, (one, two) in ((0, (p0, p1)), (2, (p2, p3))):
        for r in range(4):
            cos, sin = spectrum(fwd, jnp.concatenate([one[r], two[r]], axis=1))
            cos, sin = cos * scale, sin * scale
            for i in range(2):
                x = pos_ref[PX + e + i]
                cos_ref[x, r] = cos[:, 128 * i : 128 * i + 128]
                sin_ref[x, r] = sin[:, 128 * i : 128 * i + 128]


def conv_kernel(fwd_ref, inv_ref, kc_ref, ks_ref, p_ref, out_ref):
    fwd, inv = fwd_ref[...], inv_ref[...]
    for r in range(4):
        for x in (0, 2):
            cols = jnp.concatenate([p_ref[:, r, x].reshape(128, 128), p_ref[:, r, x + 1].reshape(128, 128)], axis=1)
            pc, ps = spectrum(fwd, cols)
            kc = jnp.concatenate([kc_ref[x, r], kc_ref[x + 1, r]], axis=1)
            ks = jnp.concatenate([ks_ref[x, r], ks_ref[x + 1, r]], axis=1)
            re = kc * pc - ks * ps
            im = kc * ps + ks * pc
            both = [re, im, HALF_ROOT * re[48:80], HALF_ROOT * im[48:80], jnp.zeros((32, 256), F32)]
            both = jnp.concatenate(both, axis=0)
            high = both.astype(BF)
            low = (both - high.astype(F32)).astype(BF)
            got = jnp.dot(inv, high, preferred_element_type=F32)
            got = (got + jnp.dot(inv, low, preferred_element_type=F32)).astype(BF)
            out_ref[:, r, x] = got[:, :128].reshape(16, 8, 128)
            out_ref[:, r, x + 1] = got[:, 128:].reshape(16, 8, 128)


def proj_kernel(pos_ref, e_ref, own, b1, lo, hi, b3, keep_ref, send_ref, buf, res):
    for x in range(4):
        for w in range(4):
            for y in range(4):
                row = 512 * x + 128 * w + 32 * y
                buf[row : row + 32] = e_ref[4 * y + w, :, x].reshape(32, 128).astype(F32)
    c = pos_ref[PC]
    for k in range(8):
        parts = [buf[pl.ds(pl.multiple_of(pos_ref[PX + j] * 512, 512) + k, 64, stride=8), :] for j in range(4)]
        left = jnp.concatenate(parts, axis=1).astype(BF)
        got = jnp.dot(left, points_of(k, own, b1, lo, hi, b3), preferred_element_type=F32)
        res[k] = got.reshape(4, 16, 256)
        for h in range(2):
            keep_ref[k, h] = res[k, 2 * h + c]
            send_ref[k, h] = res[k, 2 * h + 1 - c].astype(BF)


def body(orbitals, slab_points, kernel, twist_map):
    g, t = lax.axis_index("grp"), lax.axis_index("tw")
    x, h, c = g >> 2, (g >> 1) & 1, g & 1
    y = t >> 2
    pos = jnp.stack([x, x ^ 1, x ^ 2, x ^ 3, y, y ^ 1, y ^ 2, y ^ 3, h, c]).astype(jnp.int32)

    b1 = lax.ppermute(orbitals, "grp", XMOVE[1])
    b3 = lax.ppermute(orbitals, "grp", XMOVE[3])

    part = sds((8, 32, 256))
    far, send, hot, own = call(
        far_kernel,
        [part, part, sds((64, 384)), sds((8, 128, 256))],
        [SM, ANY, ANY],
        [pltpu.VMEM((64, 128), F32), pltpu.VMEM((4, 64), jnp.int32), pltpu.SemaphoreType.DMA((2,))],
        flops=10**8,
    )(pos, slab_points.reshape(4, 64), orbitals)
    far = far + lax.ppermute(send, "grp", CORE)
    far = lax.ppermute(far, "grp", XMOVE[2])
    pieces = call(
        split_kernel, [sds((4, 128, 128))] * 4, [SM, VM], [pltpu.VMEM((2048, 128), F32)], flops=10**9
    )(pos, kernel)
    moved = [pieces[0]]
    for e in (1, 2, 3):
        moved.append(lax.ppermute(pieces[e], "tw", YMOVE[e]))
    pieces = moved
    total, send = call(near_kernel, [part, part], [VM] * 5, flops=10**8)(hot, own, b1, b3, far)
    recv = lax.ppermute(send, "grp", CORE)
    lo = lax.ppermute(b3[:4], "grp", XMOVE[1])
    hi = lax.ppermute(b1[4:], "grp", XMOVE[3])
    total = total + recv
    from_z = lax.ppermute(total, "grp", ZSWAP)
    fwd, inv = call(table_kernel, [sds((224, 128)), sds((128, 256))], [SM], flops=10**9)(twist_map)
    from_z, fwd, inv = lax.optimization_barrier((from_z, fwd, inv))
    pieces = call(
        turn_kernel, [sds((4, 128, 128))] * 4, [SM] + [VM] * 4, [pltpu.VMEM((4, 4, 128, 128), BF)]
    )(pos, *pieces)
    moved = [pieces[0]]
    for d in (1, 2, 3):
        moved.append(lax.ppermute(pieces[d], "grp", XMOVE[d]))
    pieces = moved
    total = total + from_z
    theirs = lax.ppermute(total, "grp", CORE)
    blocks = (own, b1, lo, hi, b3)
    pairs = call(
        pair_kernel, sds((16, 4, 4, 8, 128)), [SM] + [VM] * 7, [pltpu.VMEM((2048, 128), F32)], flops=10**8
    )(pos, total, theirs, *blocks)
    owned = lax.all_to_all(pairs, "tw", split_axis=0, concat_axis=0, tiled=True)
    owned, *pieces = lax.optimization_barrier((owned, *pieces))
    kc, ks = call(kernel_spectrum, [sds((4, 4, 80, 128), F32)] * 2, [SM] + [VM] * 5, flops=10**9)(pos, fwd, *pieces)
    exchange = call(conv_kernel, sds((16, 4, 4, 8, 128)), [VM] * 5, flops=10**9)(fwd, inv, kc, ks, owned)
    rows = lax.all_to_all(exchange, "tw", split_axis=0, concat_axis=0, tiled=True)
    keep, send = call(
        proj_kernel,
        [sds((8, 2, 16, 256), F32), sds((8, 2, 16, 256))],
        [SM] + [VM] * 6,
        [pltpu.VMEM((2048, 128), F32), pltpu.VMEM((8, 4, 16, 256), F32)],
        flops=10**8,
    )(pos, rows, orbitals, *blocks[1:])
    both = keep + lax.ppermute(send, "grp", CORE).astype(F32)
    z_send = lax.dynamic_index_in_dim(both, 1 - h, 1, keepdims=False).astype(BF)
    kept = lax.dynamic_index_in_dim(both, h, 1, keepdims=False)
    return (kept + lax.ppermute(z_send, "grp", ZSWAP).astype(F32)).astype(BF)


def solution(mesh):
    return jax.shard_map(
        body,
        mesh=mesh,
        in_specs=(P("tw", "grp", None), P(), P(None, "tw", "grp"), P()),
        out_specs=P("tw", "grp", None),
        check_vma=False,
    )
```

```python
import jax
import jax.numpy as jnp
from jax import lax
from jax.experimental import pallas as pl
from jax.experimental.pallas import tpu as pltpu
from jax.sharding import PartitionSpec as P


X, H, C, Y, W = 4, 2, 2, 4, 4
HALF_ROOT = 0.7071067811865476
BF, F32 = jnp.bfloat16, jnp.float32


VM = pl.BlockSpec(memory_space=pltpu.VMEM)
SM = pl.BlockSpec(memory_space=pltpu.SMEM)
ANY = pl.BlockSpec(memory_space=pltpu.HBM)


def grp_perm(move):
    pairs = []
    for x in range(X):
        for h in range(H):
            for c in range(C):
                a, b, d = move(x, h, c)
                pairs.append(((x * H + h) * C + c, ((a % X) * H + b % H) * C + d % C))
    return pairs


CORE = grp_perm(lambda x, h, c: (x, h, c + 1))
ZSWAP = grp_perm(lambda x, h, c: (x, h + 1, c))
XMOVE = {d: grp_perm(lambda x, h, c, d=d: (x ^ d, h, c)) for d in (1, 2, 3)}
YMOVE = {e: [(t, t ^ (e * W)) for t in range(Y * W)] for e in (1, 2, 3)}

PX, PY, PH, PC = 0, 4, 8, 9


def call(kernel, outs, ins, scratch=(), flops=10**7, limit=24 << 20):
    return pl.pallas_call(
        kernel,
        out_shape=outs,
        in_specs=ins,
        out_specs=jax.tree.map(lambda _: VM, outs),
        scratch_shapes=list(scratch),
        compiler_params=pltpu.CompilerParams(vmem_limit_bytes=limit),
        cost_estimate=pl.CostEstimate(flops=flops, bytes_accessed=10**6, transcendentals=0),
    )


def sds(shape, dtype=BF):
    return jax.ShapeDtypeStruct(shape, dtype)


def far_kernel(pos_ref, pts_hbm, own_hbm, keep_ref, send_ref, hot_ref, own_ref, buf, pts_ref, sem):
    load_points = pltpu.make_async_copy(pts_hbm, pts_ref, sem.at[0])
    load_own = pltpu.make_async_copy(own_hbm, own_ref, sem.at[1])
    load_points.start()
    load_own.start()
    c = pos_ref[PC]
    sub = lax.broadcasted_iota(jnp.int32, (128, 64), 0)
    load_points.wait()

    def hot(chunk, block):
        pts = pts_ref[pl.ds(pos_ref[PX + chunk], 1)]
        base = 512 * pos_ref[PX + block] + 256 * pos_ref[PH] + 128 * c
        buf[...] = (pts == sub + base).astype(F32).T
        halves = [buf[pl.ds(pl.multiple_of(32 * i, 32), 32)] for i in (c, 1 - c)]
        return jnp.concatenate(halves, axis=0).astype(BF)

    rows = hot(2, 0)
    load_own.wait()
    for k in range(8):
        got = jnp.dot(rows, own_ref[k], preferred_element_type=F32).astype(BF)
        keep_ref[k] = got[:32]
        send_ref[k] = got[32:]
    for i, block in enumerate((0, 1, 3)):
        hot_ref[:, 128 * i : 128 * i + 128] = hot(0, block)


def near_kernel(hot_ref, own, b1, b3, far_ref, keep_ref, send_ref):
    rows = hot_ref[...]
    for k in range(8):
        points = jnp.concatenate([own[k], b1[k], b3[k]], axis=0)
        got = jnp.dot(rows, points, preferred_element_type=F32)
        keep_ref[k] = (got[:32] + far_ref[k].astype(F32)).astype(BF)
        send_ref[k] = got[32:].astype(BF)


def points_of(k, own, b1, lo, hi, b3):
    two = lo[k] if k < 4 else hi[k - 4]
    return jnp.concatenate([own[k], b1[k], two, b3[k]], axis=0)


def pair_kernel(pos_ref, mine, theirs, own, b1, lo, hi, b3, out_ref, buf):
    c = pos_ref[PC]
    for k in range(8):
        left = jnp.concatenate([mine[k], theirs[k]], axis=0)
        right = points_of(k, own, b1, lo, hi, b3)
        got = lax.dot_general(left, right, (((1,), (1,)), ((), ())), preferred_element_type=F32)
        for j in range(4):
            for i, half in enumerate((c, 1 - c)):
                base = pl.multiple_of(pos_ref[PX + j] * 512 + half * 256, 256)
                buf[pl.ds(base + k, 32, stride=8), :] = got[32 * i : 32 * i + 32, 128 * j : 128 * j + 128]
    for x in range(4):
        for w in range(4):
            for y in range(4):
                row = 512 * x + 128 * w + 32 * y
                out_ref[4 * y + w, :, x] = buf[row : row + 32].reshape(4, 8, 128).astype(BF)


def frequency(lanes):
    row = lax.broadcasted_iota(jnp.int32, (72, lanes), 0)
    fl = jnp.where(row < 12, 0, jnp.where(row < 28, 2, jnp.where(row < 40, 4, jnp.where(row < 56, 1, 3))))
    first = jnp.where(row < 12, 0, jnp.where(row < 28, 3, jnp.where(row < 40, 7, jnp.where(row < 56, 10, 14))))
    return row // 4 - first, row % 4, fl


def table_kernel(map_ref, fwd_ref, inv_ref):
    e = map_ref[0, 0]

    def neg(a):
        return map_ref[e, a]

    def add(a, b):
        return map_ref[a, neg(b)]

    def dbl(a):
        return map_ref[a, neg(a)]

    def find(ok):
        return lax.while_loop(lambda l: jnp.logical_and(l < 127, jnp.logical_not(ok(l))), lambda l: l + 1, jnp.int32(0))

    def c_ok(l):
        return dbl(dbl(l)) != e

    c = find(c_ok)
    c4 = dbl(dbl(c))

    def a_ok(l):
        d = dbl(l)
        return (dbl(d) == e) & (d != e) & (d != c4)

    a = find(a_ok)
    a2 = dbl(a)
    ac = add(a2, c4)

    def b_ok(l):
        d = dbl(l)
        return (dbl(d) == e) & (d != e) & (d != c4) & (d != a2) & (d != ac)

    b = find(b_ok)
    na, nb, nc = neg(a), neg(b), neg(c)
    lane = lax.broadcasted_iota(jnp.int32, (8, 128), 1)

    def walk(n, carry):
        start, where = carry
        cur = start
        for step in range(8):
            where = jnp.where(lane == cur, 8 * n + step, where)
            cur = map_ref[cur, nc]
        start = map_ref[start, nb]
        start = jnp.where(n % 4 == 3, map_ref[start, na], start)
        return start, where

    _, where = lax.fori_loop(0, 16, walk, (e, jnp.zeros((8, 128), jnp.int32)))
    where = where[0:1]
    li, lj, ll = where // 32, (where // 8) % 4, where % 8
    fi, fj, fl = frequency(128)
    turn = (2 * fi * li + 2 * fj * lj + fl * ll) % 8

    def parts(m):
        whole = jnp.where(m == 0, 1.0, 0.0) - jnp.where(m == 4, 1.0, 0.0)
        root = jnp.where((m == 1) | (m == 7), 1.0, 0.0) - jnp.where((m == 3) | (m == 5), 1.0, 0.0)
        return whole, root[40:72]

    cw, cr = parts(turn)
    sw, sr = parts((turn + 6) % 8)
    whole = jnp.concatenate([cw, sw, cr, sr, jnp.zeros((48, 128), F32)], axis=0)
    fwd_ref[...] = whole[0:208].astype(BF)
    inv_ref[...] = whole.T.astype(BF)


def with_root(got, root):
    return jnp.concatenate([got[0:40], got[40:72] + HALF_ROOT * root], axis=0)


def spectrum(fwd, cols):
    got = jnp.dot(fwd, cols, preferred_element_type=F32)
    return with_root(got[0:72], got[144:176]), with_root(got[72:144], got[176:208])


def split_kernel(pos_ref, k_ref, o0, o1, o2, o3, buf):
    buf[...] = k_ref[...].reshape(2048, 128).astype(F32)
    for e, ref in enumerate((o0, o1, o2, o3)):
        for r in range(4):
            ref[r] = buf[pl.ds(4 * pos_ref[PY + e] + r, 128, stride=16), :].astype(BF)


def turn_kernel(pos_ref, p0, p1, p2, p3, o0, o1, o2, o3, buf):
    for e, ref in enumerate((p0, p1, p2, p3)):
        buf[e] = ref[...]
    y = pos_ref[PY]
    for d, ref in enumerate((o0, o1, o2, o3)):
        ref[...] = buf[y ^ pos_ref[PX + d]]


def kernel_spectrum(pos_ref, fwd_ref, p0, p1, p2, p3, cos_ref, sin_ref):
    fwd = fwd_ref[...]
    fi, _, fl = frequency(256)
    alone = ((fl == 0) | (fl == 4)) & (fi != 1)
    scale = jnp.where(alone, 1.0 / 128**2, 2.0 / 128**2)
    for e, (one, two) in ((0, (p0, p1)), (2, (p2, p3))):
        for r in range(4):
            cos, sin = spectrum(fwd, jnp.concatenate([one[r], two[r]], axis=1))
            cos, sin = cos * scale, sin * scale
            for i in range(2):
                x = pos_ref[PX + e + i]
                cos_ref[x, r] = cos[:, 128 * i : 128 * i + 128].astype(BF)
                sin_ref[x, r] = sin[:, 128 * i : 128 * i + 128].astype(BF)


def conv_kernel(fwd_ref, inv_ref, kc_ref, ks_ref, p_ref, out_ref):
    fwd, inv = fwd_ref[...], inv_ref[...]
    for r in range(4):
        for x in (0, 2):
            cols = jnp.concatenate([p_ref[:, r, x].reshape(128, 128), p_ref[:, r, x + 1].reshape(128, 128)], axis=1)
            pc, ps = spectrum(fwd, cols)
            kc = jnp.concatenate([kc_ref[x, r], kc_ref[x + 1, r]], axis=1).astype(F32)
            ks = jnp.concatenate([ks_ref[x, r], ks_ref[x + 1, r]], axis=1).astype(F32)
            re = kc * pc - ks * ps
            im = kc * ps + ks * pc
            both = [re, im, HALF_ROOT * re[40:72], HALF_ROOT * im[40:72], jnp.zeros((48, 256), F32)]
            both = jnp.concatenate(both, axis=0)
            high = both.astype(BF)
            low = (both - high.astype(F32)).astype(BF)
            got = jnp.dot(inv, high, preferred_element_type=F32)
            got = (got + jnp.dot(inv, low, preferred_element_type=F32)).astype(BF)
            out_ref[:, r, x] = got[:, :128].reshape(16, 8, 128)
            out_ref[:, r, x + 1] = got[:, 128:].reshape(16, 8, 128)


def proj_kernel(pos_ref, e_ref, own, b1, lo, hi, b3, keep_ref, send_ref, buf, res):
    for x in range(4):
        for w in range(4):
            for y in range(4):
                row = 512 * x + 128 * w + 32 * y
                buf[row : row + 32] = e_ref[4 * y + w, :, x].reshape(32, 128).astype(F32)
    c = pos_ref[PC]
    for k in range(8):
        parts = [buf[pl.ds(pl.multiple_of(pos_ref[PX + j] * 512, 512) + k, 64, stride=8), :] for j in range(4)]
        left = jnp.concatenate(parts, axis=1).astype(BF)
        got = jnp.dot(left, points_of(k, own, b1, lo, hi, b3), preferred_element_type=F32)
        res[k] = got.reshape(4, 16, 256)
        for h in range(2):
            keep_ref[k, h] = res[k, 2 * h + c]
            send_ref[k, h] = res[k, 2 * h + 1 - c].astype(BF)


def body(orbitals, slab_points, kernel, twist_map):
    g, t = lax.axis_index("grp"), lax.axis_index("tw")
    x, h, c = g >> 2, (g >> 1) & 1, g & 1
    y = t >> 2
    pos = jnp.stack([x, x ^ 1, x ^ 2, x ^ 3, y, y ^ 1, y ^ 2, y ^ 3, h, c]).astype(jnp.int32)

    b1 = lax.ppermute(orbitals, "grp", XMOVE[1])
    b3 = lax.ppermute(orbitals, "grp", XMOVE[3])

    part = sds((8, 32, 256))
    far, send, hot, own = call(
        far_kernel,
        [part, part, sds((64, 384)), sds((8, 128, 256))],
        [SM, ANY, ANY],
        [pltpu.VMEM((64, 128), F32), pltpu.VMEM((4, 64), jnp.int32), pltpu.SemaphoreType.DMA((2,))],
        flops=10**8,
    )(pos, slab_points.reshape(4, 64), orbitals)
    far = far + lax.ppermute(send, "grp", CORE)
    far = lax.ppermute(far, "grp", XMOVE[2])
    pieces = call(
        split_kernel, [sds((4, 128, 128))] * 4, [SM, VM], [pltpu.VMEM((2048, 128), F32)], flops=10**9
    )(pos, kernel)
    moved = [pieces[0]]
    for e in (1, 2, 3):
        moved.append(lax.ppermute(pieces[e], "tw", YMOVE[e]))
    pieces = moved
    total, send = call(near_kernel, [part, part], [VM] * 5, flops=10**8)(hot, own, b1, b3, far)
    recv = lax.ppermute(send, "grp", CORE)
    lo = lax.ppermute(b3[:4], "grp", XMOVE[1])
    hi = lax.ppermute(b1[4:], "grp", XMOVE[3])
    total = total + recv
    from_z = lax.ppermute(total, "grp", ZSWAP)
    fwd, inv = call(table_kernel, [sds((208, 128)), sds((128, 256))], [SM], flops=10**9)(twist_map)
    from_z, fwd, inv = lax.optimization_barrier((from_z, fwd, inv))
    pieces = call(
        turn_kernel, [sds((4, 128, 128))] * 4, [SM] + [VM] * 4, [pltpu.VMEM((4, 4, 128, 128), BF)]
    )(pos, *pieces)
    moved = [pieces[0]]
    for d in (1, 2, 3):
        moved.append(lax.ppermute(pieces[d], "grp", XMOVE[d]))
    pieces = moved
    total = total + from_z
    theirs = lax.ppermute(total, "grp", CORE)
    blocks = (own, b1, lo, hi, b3)
    pairs = call(
        pair_kernel, sds((16, 4, 4, 8, 128)), [SM] + [VM] * 7, [pltpu.VMEM((2048, 128), F32)], flops=10**8
    )(pos, total, theirs, *blocks)
    owned = lax.all_to_all(pairs, "tw", split_axis=0, concat_axis=0, tiled=True)
    kc, ks = call(kernel_spectrum, [sds((4, 4, 72, 128))] * 2, [SM] + [VM] * 5, flops=10**9)(pos, fwd, *pieces)
    exchange = call(conv_kernel, sds((16, 4, 4, 8, 128)), [VM] * 5, flops=10**9)(fwd, inv, kc, ks, owned)
    rows = lax.all_to_all(exchange, "tw", split_axis=0, concat_axis=0, tiled=True)
    keep, send = call(
        proj_kernel,
        [sds((8, 2, 16, 256), F32), sds((8, 2, 16, 256))],
        [SM] + [VM] * 6,
        [pltpu.VMEM((2048, 128), F32), pltpu.VMEM((8, 4, 16, 256), F32)],
        flops=10**8,
    )(pos, rows, orbitals, *blocks[1:])
    both = keep + lax.ppermute(send, "grp", CORE).astype(F32)
    z_send = lax.dynamic_index_in_dim(both, 1 - h, 1, keepdims=False).astype(BF)
    kept = lax.dynamic_index_in_dim(both, h, 1, keepdims=False)
    return (kept + lax.ppermute(z_send, "grp", ZSWAP).astype(F32)).astype(BF)


def solution(mesh):
    return jax.shard_map(
        body,
        mesh=mesh,
        in_specs=(P("tw", "grp", None), P(), P(None, "tw", "grp"), P()),
        out_specs=P("tw", "grp", None),
        check_vma=False,
    )
```

```python
import jax
import jax.numpy as jnp
from jax import lax
from jax.experimental import pallas as pl
from jax.experimental.pallas import tpu as pltpu
from jax.sharding import PartitionSpec as P


X, H, C, Y, W = 4, 2, 2, 4, 4
HALF_ROOT = 0.7071067811865476
BF, F32 = jnp.bfloat16, jnp.float32


VM = pl.BlockSpec(memory_space=pltpu.VMEM)
SM = pl.BlockSpec(memory_space=pltpu.SMEM)
ANY = pl.BlockSpec(memory_space=pltpu.HBM)


def grp_perm(move):
    pairs = []
    for x in range(X):
        for h in range(H):
            for c in range(C):
                a, b, d = move(x, h, c)
                pairs.append(((x * H + h) * C + c, ((a % X) * H + b % H) * C + d % C))
    return pairs


CORE = grp_perm(lambda x, h, c: (x, h, c + 1))
ZSWAP = grp_perm(lambda x, h, c: (x, h + 1, c))
XMOVE = {d: grp_perm(lambda x, h, c, d=d: (x ^ d, h, c)) for d in (1, 2, 3)}
YMOVE = {e: [(t, t ^ (e * W)) for t in range(Y * W)] for e in (1, 2, 3)}

PX, PY, PH, PC = 0, 4, 8, 9


def call(kernel, outs, ins, scratch=(), flops=10**7, limit=24 << 20):
    return pl.pallas_call(
        kernel,
        out_shape=outs,
        in_specs=ins,
        out_specs=jax.tree.map(lambda _: VM, outs),
        scratch_shapes=list(scratch),
        compiler_params=pltpu.CompilerParams(vmem_limit_bytes=limit),
        cost_estimate=pl.CostEstimate(flops=flops, bytes_accessed=10**6, transcendentals=0),
    )


def sds(shape, dtype=BF):
    return jax.ShapeDtypeStruct(shape, dtype)


def far_kernel(pos_ref, pts_hbm, own_hbm, keep_ref, send_ref, hot_ref, own_ref, buf, pts_ref, sem):
    load_points = pltpu.make_async_copy(pts_hbm, pts_ref, sem.at[0])
    load_own = pltpu.make_async_copy(own_hbm, own_ref, sem.at[1])
    load_points.start()
    load_own.start()
    c = pos_ref[PC]
    sub = lax.broadcasted_iota(jnp.int32, (128, 64), 0)
    load_points.wait()

    def hot(chunk, block):
        pts = pts_ref[pl.ds(pos_ref[PX + chunk], 1)]
        base = 512 * pos_ref[PX + block] + 256 * pos_ref[PH] + 128 * c
        buf[...] = (pts == sub + base).astype(F32).T
        halves = [buf[pl.ds(pl.multiple_of(32 * i, 32), 32)] for i in (c, 1 - c)]
        return jnp.concatenate(halves, axis=0).astype(BF)

    rows = hot(2, 0)
    load_own.wait()
    for k in range(8):
        got = jnp.dot(rows, own_ref[k], preferred_element_type=F32).astype(BF)
        keep_ref[k] = got[:32]
        send_ref[k] = got[32:]
    for i, block in enumerate((0, 1, 3)):
        hot_ref[:, 128 * i : 128 * i + 128] = hot(0, block)


def near_kernel(hot_ref, own, b1, b3, far_ref, keep_ref, send_ref):
    rows = hot_ref[...]
    for k in range(8):
        points = jnp.concatenate([own[k], b1[k], b3[k]], axis=0)
        got = jnp.dot(rows, points, preferred_element_type=F32)
        keep_ref[k] = (got[:32] + far_ref[k].astype(F32)).astype(BF)
        send_ref[k] = got[32:].astype(BF)


def points_of(k, own, b1, lo, hi, b3):
    two = lo[k] if k < 4 else hi[k - 4]
    return jnp.concatenate([own[k], b1[k], two, b3[k]], axis=0)


def pair_kernel(pos_ref, mine, theirs, own, b1, lo, hi, b3, out_ref, buf):
    c = pos_ref[PC]
    for k in range(8):
        left = jnp.concatenate([mine[k], theirs[k]], axis=0)
        right = points_of(k, own, b1, lo, hi, b3)
        got = lax.dot_general(left, right, (((1,), (1,)), ((), ())), preferred_element_type=F32)
        for j in range(4):
            for i, half in enumerate((c, 1 - c)):
                base = pl.multiple_of(pos_ref[PX + j] * 512 + half * 256, 256)
                buf[pl.ds(base + k, 32, stride=8), :] = got[32 * i : 32 * i + 32, 128 * j : 128 * j + 128]
    for x in range(4):
        for w in range(4):
            for y in range(4):
                row = 512 * x + 128 * w + 32 * y
                out_ref[4 * y + w, :, x] = buf[row : row + 32].reshape(4, 8, 128).astype(BF)


def frequency(lanes):
    row = lax.broadcasted_iota(jnp.int32, (72, lanes), 0)
    fl = jnp.where(row < 12, 0, jnp.where(row < 28, 2, jnp.where(row < 40, 4, jnp.where(row < 56, 1, 3))))
    first = jnp.where(row < 12, 0, jnp.where(row < 28, 3, jnp.where(row < 40, 7, jnp.where(row < 56, 10, 14))))
    return row // 4 - first, row % 4, fl


def table_kernel(map_ref, fwd_ref, inv_ref):
    e = map_ref[0, 0]

    def neg(a):
        return map_ref[e, a]

    def add(a, b):
        return map_ref[a, neg(b)]

    def dbl(a):
        return map_ref[a, neg(a)]

    def find(ok):
        return lax.while_loop(lambda l: jnp.logical_and(l < 127, jnp.logical_not(ok(l))), lambda l: l + 1, jnp.int32(0))

    def c_ok(l):
        return dbl(dbl(l)) != e

    c = find(c_ok)
    c4 = dbl(dbl(c))

    def a_ok(l):
        d = dbl(l)
        return (dbl(d) == e) & (d != e) & (d != c4)

    a = find(a_ok)
    a2 = dbl(a)
    ac = add(a2, c4)

    def b_ok(l):
        d = dbl(l)
        return (dbl(d) == e) & (d != e) & (d != c4) & (d != a2) & (d != ac)

    b = find(b_ok)
    na, nb, nc = neg(a), neg(b), neg(c)
    lane = lax.broadcasted_iota(jnp.int32, (8, 128), 1)

    def walk(n, carry):
        start, where = carry
        cur = start
        for step in range(8):
            where = jnp.where(lane == cur, 8 * n + step, where)
            cur = map_ref[cur, nc]
        start = map_ref[start, nb]
        start = jnp.where(n % 4 == 3, map_ref[start, na], start)
        return start, where

    _, where = lax.fori_loop(0, 16, walk, (e, jnp.zeros((8, 128), jnp.int32)))
    where = where[0:1]
    li, lj, ll = where // 32, (where // 8) % 4, where % 8
    fi, fj, fl = frequency(128)
    turn = (2 * fi * li + 2 * fj * lj + fl * ll) % 8

    def parts(m):
        whole = jnp.where(m == 0, 1.0, 0.0) - jnp.where(m == 4, 1.0, 0.0)
        root = jnp.where((m == 1) | (m == 7), 1.0, 0.0) - jnp.where((m == 3) | (m == 5), 1.0, 0.0)
        return whole, root[40:72]

    cw, cr = parts(turn)
    sw, sr = parts((turn + 6) % 8)
    whole = jnp.concatenate([cw, sw, cr, sr, jnp.zeros((48, 128), F32)], axis=0)
    fwd_ref[...] = whole[0:208].astype(BF)
    inv_ref[...] = whole.T.astype(BF)


def with_root(got, root):
    return jnp.concatenate([got[0:40], got[40:72] + HALF_ROOT * root], axis=0)


def spectrum(fwd, cols):
    got = jnp.dot(fwd, cols, preferred_element_type=F32)
    return with_root(got[0:72], got[144:176]), with_root(got[72:144], got[176:208])


def split_kernel(pos_ref, k_ref, o0, o1, o2, o3, buf):
    buf[0:2048] = k_ref[...].reshape(2048, 128).astype(F32)
    for e, ref in enumerate((o0, o1, o2, o3)):
        for r in range(4):
            ref[r] = buf[pl.ds(4 * pos_ref[PY + e] + r, 128, stride=16), :].astype(BF)


def turn_kernel(pos_ref, p0, p1, p2, p3, o0, o1, o2, o3, buf):
    for e, ref in enumerate((p0, p1, p2, p3)):
        buf[e] = ref[...]
    y = pos_ref[PY]
    for d, ref in enumerate((o0, o1, o2, o3)):
        ref[...] = buf[y ^ pos_ref[PX + d]]


def kernel_spectrum(pos_ref, fwd_ref, p0, p1, p2, p3, cos_ref, sin_ref):
    fwd = fwd_ref[...]
    fi, _, fl = frequency(256)
    alone = ((fl == 0) | (fl == 4)) & (fi != 1)
    scale = jnp.where(alone, 1.0 / 128**2, 2.0 / 128**2)
    for e, (one, two) in ((0, (p0, p1)), (2, (p2, p3))):
        for r in range(4):
            cos, sin = spectrum(fwd, jnp.concatenate([one[r], two[r]], axis=1))
            cos, sin = cos * scale, sin * scale
            for i in range(2):
                x = pos_ref[PX + e + i]
                cos_ref[x, r] = cos[:, 128 * i : 128 * i + 128]
                sin_ref[x, r] = sin[:, 128 * i : 128 * i + 128].astype(BF)


def conv_kernel(fwd_ref, inv_ref, kc_ref, ks_ref, p_ref, out_ref):
    fwd, inv = fwd_ref[...], inv_ref[...]
    for r in range(4):
        for x in (0, 2):
            cols = jnp.concatenate([p_ref[:, r, x].reshape(128, 128), p_ref[:, r, x + 1].reshape(128, 128)], axis=1)
            pc, ps = spectrum(fwd, cols)
            kc = jnp.concatenate([kc_ref[x, r], kc_ref[x + 1, r]], axis=1)
            ks = jnp.concatenate([ks_ref[x, r], ks_ref[x + 1, r]], axis=1).astype(F32)
            re = kc * pc - ks * ps
            im = kc * ps + ks * pc
            both = [re, im, HALF_ROOT * re[40:72], HALF_ROOT * im[40:72], jnp.zeros((48, 256), F32)]
            both = jnp.concatenate(both, axis=0)
            high = both.astype(BF)
            low = (both - high.astype(F32)).astype(BF)
            got = jnp.dot(inv, high, preferred_element_type=F32)
            got = (got + jnp.dot(inv, low, preferred_element_type=F32)).astype(BF)
            out_ref[:, r, x] = got[:, :128].reshape(16, 8, 128)
            out_ref[:, r, x + 1] = got[:, 128:].reshape(16, 8, 128)


def proj_kernel(pos_ref, e_ref, own, b1, lo, hi, b3, keep_ref, send_ref, buf, res):
    for x in range(4):
        for w in range(4):
            for y in range(4):
                row = 512 * x + 128 * w + 32 * y
                buf[row : row + 32] = e_ref[4 * y + w, :, x].reshape(32, 128).astype(F32)
    c = pos_ref[PC]
    for k in range(8):
        parts = [buf[pl.ds(pl.multiple_of(pos_ref[PX + j] * 512, 512) + k, 64, stride=8), :] for j in range(4)]
        left = jnp.concatenate(parts, axis=1).astype(BF)
        got = jnp.dot(left, points_of(k, own, b1, lo, hi, b3), preferred_element_type=F32)
        res[k] = got.reshape(4, 16, 256)
        for h in range(2):
            keep_ref[k, h] = res[k, 2 * h + c]
            send_ref[k, h] = res[k, 2 * h + 1 - c].astype(BF)


def body(orbitals, slab_points, kernel, twist_map):
    g, t = lax.axis_index("grp"), lax.axis_index("tw")
    x, h, c = g >> 2, (g >> 1) & 1, g & 1
    y = t >> 2
    pos = jnp.stack([x, x ^ 1, x ^ 2, x ^ 3, y, y ^ 1, y ^ 2, y ^ 3, h, c]).astype(jnp.int32)

    b1 = lax.ppermute(orbitals, "grp", XMOVE[1])
    b3 = lax.ppermute(orbitals, "grp", XMOVE[3])

    part = sds((8, 32, 256))
    far, send, hot, own = call(
        far_kernel,
        [part, part, sds((64, 384)), sds((8, 128, 256))],
        [SM, ANY, ANY],
        [pltpu.VMEM((64, 128), F32), pltpu.VMEM((4, 64), jnp.int32), pltpu.SemaphoreType.DMA((2,))],
        flops=10**8,
    )(pos, slab_points.reshape(4, 64), orbitals)
    far = far + lax.ppermute(send, "grp", CORE)
    far = lax.ppermute(far, "grp", XMOVE[2])
    pieces = call(
        split_kernel, [sds((4, 128, 128))] * 4, [SM, VM], [pltpu.VMEM((2064, 128), F32)], flops=10**9
    )(pos, kernel)
    moved = [pieces[0]]
    for e in (1, 2, 3):
        moved.append(lax.ppermute(pieces[e], "tw", YMOVE[e]))
    pieces = moved
    total, send = call(near_kernel, [part, part], [VM] * 5, flops=10**8)(hot, own, b1, b3, far)
    recv = lax.ppermute(send, "grp", CORE)
    lo = lax.ppermute(b3[:4], "grp", XMOVE[1])
    hi = lax.ppermute(b1[4:], "grp", XMOVE[3])
    total = total + recv
    from_z = lax.ppermute(total, "grp", ZSWAP)
    fwd, inv = call(table_kernel, [sds((208, 128)), sds((128, 256))], [SM], flops=10**9)(twist_map)
    from_z, fwd, inv = lax.optimization_barrier((from_z, fwd, inv))
    pieces = call(
        turn_kernel, [sds((4, 128, 128))] * 4, [SM] + [VM] * 4, [pltpu.VMEM((4, 4, 128, 128), BF)]
    )(pos, *pieces)
    moved = [pieces[0]]
    for d in (1, 2, 3):
        moved.append(lax.ppermute(pieces[d], "grp", XMOVE[d]))
    pieces = moved
    total = total + from_z
    theirs = lax.ppermute(total, "grp", CORE)
    blocks = (own, b1, lo, hi, b3)
    pairs = call(
        pair_kernel, sds((16, 4, 4, 8, 128)), [SM] + [VM] * 7, [pltpu.VMEM((2064, 128), F32)], flops=10**8
    )(pos, total, theirs, *blocks)
    owned = lax.all_to_all(pairs, "tw", split_axis=0, concat_axis=0, tiled=True)
    kc, ks = call(
        kernel_spectrum, [sds((4, 4, 72, 128), F32), sds((4, 4, 72, 128))], [SM] + [VM] * 5, flops=10**9
    )(pos, fwd, *pieces)
    exchange = call(conv_kernel, sds((16, 4, 4, 8, 128)), [VM] * 5, flops=10**9)(fwd, inv, kc, ks, owned)
    rows = lax.all_to_all(exchange, "tw", split_axis=0, concat_axis=0, tiled=True)
    keep, send = call(
        proj_kernel,
        [sds((8, 2, 16, 256), F32), sds((8, 2, 16, 256))],
        [SM] + [VM] * 6,
        [pltpu.VMEM((2064, 128), F32), pltpu.VMEM((8, 4, 16, 256), F32)],
        flops=10**8,
    )(pos, rows, orbitals, *blocks[1:])
    both = keep + lax.ppermute(send, "grp", CORE).astype(F32)
    z_send = lax.dynamic_index_in_dim(both, 1 - h, 1, keepdims=False).astype(BF)
    kept = lax.dynamic_index_in_dim(both, h, 1, keepdims=False)
    return (kept + lax.ppermute(z_send, "grp", ZSWAP).astype(F32)).astype(BF)


def solution(mesh):
    return jax.shard_map(
        body,
        mesh=mesh,
        in_specs=(P("tw", "grp", None), P(), P(None, "tw", "grp"), P()),
        out_specs=P("tw", "grp", None),
        check_vma=False,
    )
```

```python
import jax
import jax.numpy as jnp
from jax import lax
from jax.experimental import pallas as pl
from jax.experimental.pallas import tpu as pltpu
from jax.sharding import PartitionSpec as P


X, H, C, Y, W = 4, 2, 2, 4, 4
HALF_ROOT = 0.7071067811865476
BF, F32 = jnp.bfloat16, jnp.float32


VM = pl.BlockSpec(memory_space=pltpu.VMEM)
SM = pl.BlockSpec(memory_space=pltpu.SMEM)
ANY = pl.BlockSpec(memory_space=pltpu.HBM)


def grp_perm(move):
    pairs = []
    for x in range(X):
        for h in range(H):
            for c in range(C):
                a, b, d = move(x, h, c)
                pairs.append(((x * H + h) * C + c, ((a % X) * H + b % H) * C + d % C))
    return pairs


CORE = grp_perm(lambda x, h, c: (x, h, c + 1))
ZSWAP = grp_perm(lambda x, h, c: (x, h + 1, c))
XMOVE = {d: grp_perm(lambda x, h, c, d=d: (x ^ d, h, c)) for d in (1, 2, 3)}
YMOVE = {e: [(t, t ^ (e * W)) for t in range(Y * W)] for e in (1, 2, 3)}

PX, PY, PH, PC = 0, 4, 8, 9


def call(kernel, outs, ins, scratch=(), flops=10**7, limit=24 << 20):
    return pl.pallas_call(
        kernel,
        out_shape=outs,
        in_specs=ins,
        out_specs=jax.tree.map(lambda _: VM, outs),
        scratch_shapes=list(scratch),
        compiler_params=pltpu.CompilerParams(vmem_limit_bytes=limit),
        cost_estimate=pl.CostEstimate(flops=flops, bytes_accessed=10**6, transcendentals=0),
    )


def sds(shape, dtype=BF):
    return jax.ShapeDtypeStruct(shape, dtype)


def far_kernel(pos_ref, pts_hbm, own_hbm, keep_ref, send_ref, own_ref, buf, pts_ref, sem):
    load_points = pltpu.make_async_copy(pts_hbm, pts_ref, sem.at[0])
    load_own = pltpu.make_async_copy(own_hbm, own_ref, sem.at[1])
    load_points.start()
    load_own.start()
    c = pos_ref[PC]
    sub = lax.broadcasted_iota(jnp.int32, (128, 64), 0)
    load_points.wait()

    def hot(chunk, block):
        pts = pts_ref[pl.ds(pos_ref[PX + chunk], 1)]
        base = 512 * pos_ref[PX + block] + 256 * pos_ref[PH] + 128 * c
        buf[...] = (pts == sub + base).astype(F32).T
        halves = [buf[pl.ds(pl.multiple_of(32 * i, 32), 32)] for i in (c, 1 - c)]
        return jnp.concatenate(halves, axis=0).astype(BF)

    rows = hot(2, 0)
    load_own.wait()
    for k in range(8):
        got = jnp.dot(rows, own_ref[k], preferred_element_type=F32).astype(BF)
        keep_ref[k] = got[:32]
        send_ref[k] = got[32:]


def hot_kernel(pos_ref, pts_ref, hot_ref, buf):
    c = pos_ref[PC]
    sub = lax.broadcasted_iota(jnp.int32, (128, 64), 0)

    def hot(chunk, block):
        pts = pts_ref[pl.ds(pos_ref[PX + chunk], 1)]
        base = 512 * pos_ref[PX + block] + 256 * pos_ref[PH] + 128 * c
        buf[...] = (pts == sub + base).astype(F32).T
        halves = [buf[pl.ds(pl.multiple_of(32 * i, 32), 32)] for i in (c, 1 - c)]
        return jnp.concatenate(halves, axis=0).astype(BF)

    for i, block in enumerate((0, 1, 3)):
        hot_ref[:, 128 * i : 128 * i + 128] = hot(0, block)


def near_kernel(hot_ref, own, b1, b3, far_ref, keep_ref, send_ref):
    rows = hot_ref[...]
    for k in range(8):
        points = jnp.concatenate([own[k], b1[k], b3[k]], axis=0)
        got = jnp.dot(rows, points, preferred_element_type=F32)
        keep_ref[k] = (got[:32] + far_ref[k].astype(F32)).astype(BF)
        send_ref[k] = got[32:].astype(BF)


def points_of(k, own, b1, lo, hi, b3):
    two = lo[k] if k < 4 else hi[k - 4]
    return jnp.concatenate([own[k], b1[k], two, b3[k]], axis=0)


def pair_kernel(pos_ref, mine, theirs, own, b1, lo, hi, b3, out_ref, buf):
    c = pos_ref[PC]
    for k in range(8):
        left = jnp.concatenate([mine[k], theirs[k]], axis=0)
        right = points_of(k, own, b1, lo, hi, b3)
        got = lax.dot_general(left, right, (((1,), (1,)), ((), ())), preferred_element_type=F32)
        for j in range(4):
            for i, half in enumerate((c, 1 - c)):
                base = pl.multiple_of(pos_ref[PX + j] * 512 + half * 256, 256)
                buf[pl.ds(base + k, 32, stride=8), :] = got[32 * i : 32 * i + 32, 128 * j : 128 * j + 128]
    for x in range(4):
        for w in range(4):
            for y in range(4):
                row = 512 * x + 128 * w + 32 * y
                out_ref[4 * y + w, :, x] = buf[row : row + 32].reshape(4, 8, 128).astype(BF)


def frequency(lanes):
    row = lax.broadcasted_iota(jnp.int32, (72, lanes), 0)
    fl = jnp.where(row < 12, 0, jnp.where(row < 28, 2, jnp.where(row < 40, 4, jnp.where(row < 56, 1, 3))))
    first = jnp.where(row < 12, 0, jnp.where(row < 28, 3, jnp.where(row < 40, 7, jnp.where(row < 56, 10, 14))))
    return row // 4 - first, row % 4, fl


def table_kernel(map_ref, fwd_ref, inv_ref):
    e = map_ref[0, 0]

    def neg(a):
        return map_ref[e, a]

    def add(a, b):
        return map_ref[a, neg(b)]

    def dbl(a):
        return map_ref[a, neg(a)]

    def find(ok):
        return lax.while_loop(lambda l: jnp.logical_and(l < 127, jnp.logical_not(ok(l))), lambda l: l + 1, jnp.int32(0))

    def c_ok(l):
        return dbl(dbl(l)) != e

    c = find(c_ok)
    c4 = dbl(dbl(c))

    def a_ok(l):
        d = dbl(l)
        return (dbl(d) == e) & (d != e) & (d != c4)

    a = find(a_ok)
    a2 = dbl(a)
    ac = add(a2, c4)

    def b_ok(l):
        d = dbl(l)
        return (dbl(d) == e) & (d != e) & (d != c4) & (d != a2) & (d != ac)

    b = find(b_ok)
    na, nb, nc = neg(a), neg(b), neg(c)
    lane = lax.broadcasted_iota(jnp.int32, (8, 128), 1)

    def walk(n, carry):
        start, where = carry
        cur = start
        for step in range(8):
            where = jnp.where(lane == cur, 8 * n + step, where)
            cur = map_ref[cur, nc]
        start = map_ref[start, nb]
        start = jnp.where(n % 4 == 3, map_ref[start, na], start)
        return start, where

    _, where = lax.fori_loop(0, 16, walk, (e, jnp.zeros((8, 128), jnp.int32)))
    where = where[0:1]
    li, lj, ll = where // 32, (where // 8) % 4, where % 8
    fi, fj, fl = frequency(128)
    turn = (2 * fi * li + 2 * fj * lj + fl * ll) % 8

    def parts(m):
        whole = jnp.where(m == 0, 1.0, 0.0) - jnp.where(m == 4, 1.0, 0.0)
        root = jnp.where((m == 1) | (m == 7), 1.0, 0.0) - jnp.where((m == 3) | (m == 5), 1.0, 0.0)
        return whole, root[40:72]

    cw, cr = parts(turn)
    sw, sr = parts((turn + 6) % 8)
    whole = jnp.concatenate([cw, sw, cr, sr, jnp.zeros((48, 128), F32)], axis=0)
    fwd_ref[...] = whole[0:208].astype(BF)
    inv_ref[...] = whole.T.astype(BF)


def with_root(got, root):
    return jnp.concatenate([got[0:40], got[40:72] + HALF_ROOT * root], axis=0)


def spectrum(fwd, cols):
    got = jnp.dot(fwd, cols, preferred_element_type=F32)
    return with_root(got[0:72], got[144:176]), with_root(got[72:144], got[176:208])


def split_kernel(pos_ref, k_ref, o0, o1, o2, o3, buf):
    buf[0:2048] = k_ref[...].reshape(2048, 128).astype(F32)
    for e, ref in enumerate((o0, o1, o2, o3)):
        for r in range(4):
            ref[r] = buf[pl.ds(4 * pos_ref[PY + e] + r, 128, stride=16), :].astype(BF)


def turn_kernel(pos_ref, p0, p1, p2, p3, o0, o1, o2, o3, buf):
    for e, ref in enumerate((p0, p1, p2, p3)):
        buf[e] = ref[...]
    y = pos_ref[PY]
    for d, ref in enumerate((o0, o1, o2, o3)):
        ref[...] = buf[y ^ pos_ref[PX + d]]


def kernel_spectrum(pos_ref, fwd_ref, p0, p1, p2, p3, cos_ref, sin_ref):
    fwd = fwd_ref[...]
    fi, _, fl = frequency(256)
    alone = ((fl == 0) | (fl == 4)) & (fi != 1)
    scale = jnp.where(alone, 1.0 / 128**2, 2.0 / 128**2)
    for e, (one, two) in ((0, (p0, p1)), (2, (p2, p3))):
        for r in range(4):
            cos, sin = spectrum(fwd, jnp.concatenate([one[r], two[r]], axis=1))
            cos, sin = cos * scale, sin * scale
            for i in range(2):
                x = pos_ref[PX + e + i]
                cos_ref[x, r] = cos[:, 128 * i : 128 * i + 128]
                sin_ref[x, r] = sin[:, 128 * i : 128 * i + 128].astype(BF)


def conv_kernel(fwd_ref, inv_ref, kc_ref, ks_ref, p_ref, out_ref):
    fwd, inv = fwd_ref[...], inv_ref[...]
    for r in range(4):
        for x in (0, 2):
            cols = jnp.concatenate([p_ref[:, r, x].reshape(128, 128), p_ref[:, r, x + 1].reshape(128, 128)], axis=1)
            pc, ps = spectrum(fwd, cols)
            kc = jnp.concatenate([kc_ref[x, r], kc_ref[x + 1, r]], axis=1)
            ks = jnp.concatenate([ks_ref[x, r], ks_ref[x + 1, r]], axis=1).astype(F32)
            re = kc * pc - ks * ps
            im = kc * ps + ks * pc
            both = [re, im, HALF_ROOT * re[40:72], HALF_ROOT * im[40:72], jnp.zeros((48, 256), F32)]
            both = jnp.concatenate(both, axis=0)
            high = both.astype(BF)
            low = (both - high.astype(F32)).astype(BF)
            got = jnp.dot(inv, high, preferred_element_type=F32)
            got = (got + jnp.dot(inv, low, preferred_element_type=F32)).astype(BF)
            out_ref[:, r, x] = got[:, :128].reshape(16, 8, 128)
            out_ref[:, r, x + 1] = got[:, 128:].reshape(16, 8, 128)


def proj_kernel(pos_ref, e_ref, own, b1, lo, hi, b3, keep_ref, send_ref, buf, res):
    for x in range(4):
        for w in range(4):
            for y in range(4):
                row = 512 * x + 128 * w + 32 * y
                buf[row : row + 32] = e_ref[4 * y + w, :, x].reshape(32, 128).astype(F32)
    c = pos_ref[PC]
    for k in range(8):
        parts = [buf[pl.ds(pl.multiple_of(pos_ref[PX + j] * 512, 512) + k, 64, stride=8), :] for j in range(4)]
        left = jnp.concatenate(parts, axis=1).astype(BF)
        got = jnp.dot(left, points_of(k, own, b1, lo, hi, b3), preferred_element_type=F32)
        res[k] = got.reshape(4, 16, 256)
        for h in range(2):
            keep_ref[k, h] = res[k, 2 * h + c]
            send_ref[k, h] = res[k, 2 * h + 1 - c].astype(BF)


def body(orbitals, slab_points, kernel, twist_map):
    g, t = lax.axis_index("grp"), lax.axis_index("tw")
    x, h, c = g >> 2, (g >> 1) & 1, g & 1
    y = t >> 2
    pos = jnp.stack([x, x ^ 1, x ^ 2, x ^ 3, y, y ^ 1, y ^ 2, y ^ 3, h, c]).astype(jnp.int32)

    b1 = lax.ppermute(orbitals, "grp", XMOVE[1])
    b3 = lax.ppermute(orbitals, "grp", XMOVE[3])

    part = sds((8, 32, 256))
    far, send, own = call(
        far_kernel,
        [part, part, sds((8, 128, 256))],
        [SM, ANY, ANY],
        [pltpu.VMEM((64, 128), F32), pltpu.VMEM((4, 64), jnp.int32), pltpu.SemaphoreType.DMA((2,))],
        flops=10**8,
    )(pos, slab_points.reshape(4, 64), orbitals)
    far = far + lax.ppermute(send, "grp", CORE)
    far = lax.ppermute(far, "grp", XMOVE[2])
    hot = call(hot_kernel, sds((64, 384)), [SM, VM], [pltpu.VMEM((64, 128), F32)])(pos, slab_points.reshape(4, 64))
    pieces = call(
        split_kernel, [sds((4, 128, 128))] * 4, [SM, VM], [pltpu.VMEM((2064, 128), F32)], flops=10**9
    )(pos, kernel)
    moved = [pieces[0]]
    for e in (1, 2, 3):
        moved.append(lax.ppermute(pieces[e], "tw", YMOVE[e]))
    pieces = moved
    total, send = call(near_kernel, [part, part], [VM] * 5, flops=10**8)(hot, own, b1, b3, far)
    recv = lax.ppermute(send, "grp", CORE)
    lo = lax.ppermute(b3[:4], "grp", XMOVE[1])
    hi = lax.ppermute(b1[4:], "grp", XMOVE[3])
    total = total + recv
    from_z = lax.ppermute(total, "grp", ZSWAP)
    fwd, inv = call(table_kernel, [sds((208, 128)), sds((128, 256))], [SM], flops=10**9)(twist_map)
    from_z, fwd, inv = lax.optimization_barrier((from_z, fwd, inv))
    pieces = call(
        turn_kernel, [sds((4, 128, 128))] * 4, [SM] + [VM] * 4, [pltpu.VMEM((4, 4, 128, 128), BF)]
    )(pos, *pieces)
    moved = [pieces[0]]
    for d in (1, 2, 3):
        moved.append(lax.ppermute(pieces[d], "grp", XMOVE[d]))
    pieces = moved
    total = total + from_z
    theirs = lax.ppermute(total, "grp", CORE)
    blocks = (own, b1, lo, hi, b3)
    pairs = call(
        pair_kernel, sds((16, 4, 4, 8, 128)), [SM] + [VM] * 7, [pltpu.VMEM((2064, 128), F32)], flops=10**8
    )(pos, total, theirs, *blocks)
    owned = lax.all_to_all(pairs, "tw", split_axis=0, concat_axis=0, tiled=True)
    kc, ks = call(
        kernel_spectrum, [sds((4, 4, 72, 128), F32), sds((4, 4, 72, 128))], [SM] + [VM] * 5, flops=10**9
    )(pos, fwd, *pieces)
    exchange = call(conv_kernel, sds((16, 4, 4, 8, 128)), [VM] * 5, flops=10**9)(fwd, inv, kc, ks, owned)
    rows = lax.all_to_all(exchange, "tw", split_axis=0, concat_axis=0, tiled=True)
    keep, send = call(
        proj_kernel,
        [sds((8, 2, 16, 256), F32), sds((8, 2, 16, 256))],
        [SM] + [VM] * 6,
        [pltpu.VMEM((2064, 128), F32), pltpu.VMEM((8, 4, 16, 256), F32)],
        flops=10**8,
    )(pos, rows, orbitals, *blocks[1:])
    both = keep + lax.ppermute(send, "grp", CORE).astype(F32)
    z_send = lax.dynamic_index_in_dim(both, 1 - h, 1, keepdims=False).astype(BF)
    kept = lax.dynamic_index_in_dim(both, h, 1, keepdims=False)
    return (kept + lax.ppermute(z_send, "grp", ZSWAP).astype(F32)).astype(BF)


def solution(mesh):
    return jax.shard_map(
        body,
        mesh=mesh,
        in_specs=(P("tw", "grp", None), P(), P(None, "tw", "grp"), P()),
        out_specs=P("tw", "grp", None),
        check_vma=False,
    )
```
